256 devices in a mesh: cls: 16 (over y, x), batch: 16 (over z, core).
Axes of the slice: x: 4, y: 4, z: 8, core: 2. Of those that a mesh axis runs over, the one named last changes fastest.
Arguments:
- particles: bfloat16 [2048, 5120, 128], P('batch', 'cls'), may hold values from -6 to 6
- volumes: bfloat16 [16, 5120, 128], P('batch', 'cls'), may hold values from -6 to 6
- assignment: int32 [2048], P('batch'), may hold values from 0 to 15
- defocus: float32 [2048], P('batch'), may hold values from 1 to 8
- tilt_limits: int32 [2048, 2], P('batch'), may hold values from 2 to 16
- orientation: int32 [2048], P('batch'), may hold values from 0 to 7
Outputs:
- updated: float32 [16, 5120, 128], P('batch', 'cls')
- scores: float32 [2048], P('batch')
The draws below stay inside these ranges and needn't reach their ends.
All inputs are finite; a program needn't handle non-finite values.
Results may differ from the reference program's by a relative error of at most 0.0015.
Values may be sent and summed in bfloat16 or wider, within the bound.
A program may use at most 128 MiB of HBM per device.

```python
import math
import jax
import jax.numpy as jnp
import numpy as np
from jax import lax

CLASSES = 16
LENGTH = 128
ORIENTS = 8
LINES = 5120
PARTICLES = 2048


noise_level = 0.45


phase_offset = 0.1


def volume_field(key):
    seed_key = jax.random.fold_in(key, 101)
    values = jax.random.truncated_normal(seed_key, -6.0, 6.0, (CLASSES, LINES, LENGTH), jnp.float32)
    return values.astype(jnp.bfloat16)


def class_field(key):
    ranking_key = jax.random.fold_in(key, 202)
    lottery_key = jax.random.fold_in(key, 203)
    ranking = jax.random.permutation(ranking_key, CLASSES).astype(jnp.int32)
    common_weight = math.lcm(*range(1, CLASSES + 1))
    weights = np.array([common_weight // (number + 1) for number in range(CLASSES)], dtype=np.int64)
    bounds_table = np.cumsum(weights)
    total_weight = int(bounds_table[-1])
    bounds = jnp.asarray(bounds_table.astype(np.int32))
    lottery = jax.random.randint(lottery_key, (PARTICLES,), 0, total_weight, dtype=jnp.int32)
    positions = jnp.sum((lottery[:, None] >= bounds[None, :]).astype(jnp.int32), axis=1)
    return ranking[positions].astype(jnp.int32)


def defocus_field(key):
    seed_key = jax.random.fold_in(key, 303)
    values = jnp.exp(jax.random.uniform(seed_key, (PARTICLES,), jnp.float32, 0.0, math.log(8.0)))
    return jnp.clip(values, 1.0, 8.0)


def tilt_field(key):
    return jax.random.randint(jax.random.fold_in(key, 404), (PARTICLES, 2), 2, 17, dtype=jnp.int32)


def orient_field(key):
    return jax.random.randint(jax.random.fold_in(key, 505), (PARTICLES,), 0, ORIENTS, dtype=jnp.int32)


def draw_volumes(key, part):
    return volume_field(key)


def draw_assignment(key, part):
    return class_field(key)


def draw_defocus(key, part):
    return defocus_field(key)


def draw_tilt_limits(key, part):
    return tilt_field(key)


def draw_orientation(key, part):
    return orient_field(key)


def draw_particles(key, part):
    volume_values = volume_field(key).astype(jnp.float32)
    indices = jnp.arange(LENGTH, dtype=jnp.int32)
    angle = 2.0 * math.pi * (indices[:, None] * indices[None, :] % LENGTH).astype(jnp.float32) / LENGTH
    forward_table = jnp.concatenate([jnp.cos(angle), -jnp.sin(angle)], axis=1)
    back_table = jnp.concatenate([jnp.cos(angle), -jnp.sin(angle)], axis=0) / LENGTH
    spectra = jnp.dot(volume_values.reshape(CLASSES * LINES, LENGTH), forward_table, precision=lax.Precision.HIGHEST)
    spectra = spectra.reshape(CLASSES, LINES, 2 * LENGTH)
    classes_of = class_field(key)
    defocus_all = defocus_field(key)
    tilts_all = tilt_field(key)
    orients_all = orient_field(key)
    half_length = LENGTH // 2
    signed = jnp.where(indices < half_length, indices, indices - LENGTH)
    radius = 1 + jnp.arange(LINES, dtype=jnp.int32) % half_length
    radial = (signed[None, :] * signed[None, :] + radius[:, None] * radius[:, None]).astype(jnp.float32) / float(half_length * half_length)
    sgrid = signed[None, None, :]
    rgrid = radius[None, :, None]
    block_size = 16
    blocks = PARTICLES // block_size
    noise_key = jax.random.fold_in(key, 606)

    def one_block(number):
        start = number * block_size
        picked = lax.dynamic_slice_in_dim(classes_of, start, block_size)
        defocus_block = lax.dynamic_slice_in_dim(defocus_all, start, block_size)
        tilt_block = lax.dynamic_slice_in_dim(tilts_all, start, block_size)
        orient_block = lax.dynamic_slice_in_dim(orients_all, start, block_size)
        contrast = -jnp.sin(math.pi * defocus_block[:, None, None] * radial[None, :, :] + phase_offset)
        plus = tilt_block[:, 0][:, None, None]
        minus = tilt_block[:, 1][:, None, None]
        keep_here = jnp.where(sgrid >= 0, 8 * sgrid <= plus * rgrid, -8 * sgrid <= minus * rgrid)
        keep_mirror = jnp.where(sgrid <= 0, -8 * sgrid <= plus * rgrid, 8 * sgrid <= minus * rgrid)
        amplitude = contrast * 0.5 * (keep_here.astype(jnp.float32) + keep_mirror.astype(jnp.float32))
        shifts = orient_block * (LENGTH // ORIENTS)
        phase_turn = 2.0 * math.pi * (indices[None, :] * shifts[:, None] % LENGTH).astype(jnp.float32) / LENGTH
        filter_real = amplitude * jnp.cos(phase_turn)[:, None, :]
        filter_imag = -amplitude * jnp.sin(phase_turn)[:, None, :]
        chosen = spectra[picked]
        volume_real = chosen[:, :, :LENGTH]
        volume_imag = chosen[:, :, LENGTH:]
        spec_real = filter_real * volume_real - filter_imag * volume_imag
        spec_imag = filter_real * volume_imag + filter_imag * volume_real
        joined = jnp.concatenate([spec_real, spec_imag], axis=2).reshape(block_size * LINES, 2 * LENGTH)
        signal = jnp.dot(joined, back_table, precision=lax.Precision.HIGHEST).reshape(block_size, LINES, LENGTH)
        block_key = jax.random.fold_in(noise_key, number)
        noise = noise_level * jax.random.normal(block_key, (block_size, LINES, LENGTH), jnp.float32)
        return jnp.clip(signal + noise, -6.0, 6.0).astype(jnp.bfloat16)
    result = lax.map(one_block, jnp.arange(blocks, dtype=jnp.int32))
    return result.reshape(PARTICLES, LINES, LENGTH)


def setup_inputs(seed: int = 0) -> dict:
    seeds = jax.random.split(jax.random.key(seed), 7)
    return {
        "particles": draw_particles(jax.random.fold_in(seeds[6], 71), 0),
        "volumes": draw_volumes(jax.random.fold_in(seeds[6], 71), 0),
        "assignment": draw_assignment(jax.random.fold_in(seeds[6], 71), 0),
        "defocus": draw_defocus(jax.random.fold_in(seeds[6], 71), 0),
        "tilt_limits": draw_tilt_limits(jax.random.fold_in(seeds[6], 71), 0),
        "orientation": draw_orientation(jax.random.fold_in(seeds[6], 71), 0),
    }


step_size = 0.5
phase_offset = 0.1


def make_tables(line_length):
    index = jnp.arange(line_length, dtype=jnp.int32)
    angle = 2.0 * math.pi * ((index[:, None] * index[None, :]) % line_length).astype(jnp.float32) / line_length
    cosine = jnp.cos(angle)
    sine = jnp.sin(angle)
    forward_model = jnp.concatenate([cosine, -sine], axis=1).astype(jnp.bfloat16)
    back = jnp.concatenate([cosine, -sine], axis=0) / line_length
    return forward_model, back


def make_filters(defocus, tilt_limits, orientation, radius, line_length, orients):
    freq = jnp.arange(line_length, dtype=jnp.int32)
    signed = jnp.where(freq < line_length // 2, freq, freq - line_length)
    half = line_length // 2
    along_s = math.pi * defocus[:, None] * ((signed * signed).astype(jnp.float32) / float(half * half))[None, :] + phase_offset
    along_r = math.pi * defocus[:, None] * ((radius * radius).astype(jnp.float32) / float(half * half))[None, :]
    ctf = -(jnp.sin(along_s)[:, None, :] * jnp.cos(along_r)[:, :, None] + jnp.cos(along_s)[:, None, :] * jnp.sin(along_r)[:, :, None])
    plus = tilt_limits[:, 0][:, None, None]
    minus = tilt_limits[:, 1][:, None, None]
    sgrid = signed[None, None, :]
    rgrid = radius[None, :, None]
    keep = jnp.where(sgrid >= 0, 8 * sgrid <= plus * rgrid, -8 * sgrid <= minus * rgrid)
    amp = ctf * keep.astype(jnp.float32)
    shift = orientation * (line_length // orients)
    turn = 2.0 * math.pi * ((freq[None, :] * shift[:, None]) % line_length).astype(jnp.float32) / line_length
    filtered_real = amp * jnp.cos(turn)[:, None, :]
    filtered_imaginary = -amp * jnp.sin(turn)[:, None, :]
    return filtered_real, filtered_imaginary


def reference(particles, volumes, assignment, defocus, tilt_limits, orientation):
    forward_model, back = make_tables(LENGTH)
    classes, line_rows, line_length = volumes.shape
    total = particles.shape[0]
    spectra = jnp.dot(volumes.reshape(classes * line_rows, line_length), forward_model, preferred_element_type=jnp.float32)
    spectra = spectra.astype(jnp.bfloat16).reshape(classes, line_rows, 2 * line_length)
    radius = 1 + jnp.arange(line_rows, dtype=jnp.int32) % (line_length // 2)
    block_range = math.gcd(total, 64)
    count = total // block_range
    scale = 1.0 / (line_rows * line_length * line_length)

    def step(carry, items):
        sums, counts = carry
        group_spectra, group_a, group_d, group_t, group_o = items
        spectrum_estimate = jnp.dot(group_spectra.reshape(block_range * line_rows, line_length), forward_model, preferred_element_type=jnp.float32)
        spectrum_estimate = spectrum_estimate.reshape(block_range, line_rows, 2 * line_length)
        chosen_class = spectra[group_a].astype(jnp.float32)
        filtered_real, filtered_imaginary = make_filters(group_d, group_t, group_o, radius, line_length, ORIENTS)
        volume_real = chosen_class[:, :, :line_length]
        volume_imaginary = chosen_class[:, :, line_length:]
        residual_real = spectrum_estimate[:, :, :line_length] - (filtered_real * volume_real - filtered_imaginary * volume_imaginary)
        residual_imaginary = spectrum_estimate[:, :, line_length:] - (filtered_real * volume_imaginary + filtered_imaginary * volume_real)
        score = jnp.sum(residual_real * residual_real + residual_imaginary * residual_imaginary, axis=(1, 2)) * scale
        grads = jnp.concatenate([filtered_real * residual_real + filtered_imaginary * residual_imaginary, filtered_real * residual_imaginary - filtered_imaginary * residual_real], axis=2)
        onehot = (group_a[:, None] == jnp.arange(classes, dtype=jnp.int32)[None, :]).astype(jnp.float32)
        sums = sums + jnp.einsum("bk,bgf->kgf", onehot, grads, precision=lax.Precision.HIGHEST)
        counts = counts + jnp.sum(onehot, axis=0)
        return (sums, counts), score

    items = (particles.reshape(count, block_range, line_rows, line_length), assignment.reshape(count, block_range),
             defocus.reshape(count, block_range), tilt_limits.reshape(count, block_range, 2), orientation.reshape(count, block_range))
    start = (jnp.zeros((classes, line_rows, 2 * line_length), jnp.float32), jnp.zeros((classes,), jnp.float32))
    (sums, counts), scores = lax.scan(step, start, items)
    grad = jnp.dot(sums.reshape(classes * line_rows, 2 * line_length), back, precision=lax.Precision.HIGHEST,
                   preferred_element_type=jnp.float32).reshape(classes, line_rows, line_length)
    updated = volumes.astype(jnp.float32) + step_size * grad / (counts + 1.0)[:, None, None]
    return updated, scores.reshape(total)
```

```python
import math

import jax
import jax.numpy as jnp
import numpy as np
from jax import lax
from jax.experimental import pallas as pl
from jax.experimental.pallas import tpu as pltpu
from jax.sharding import PartitionSpec as P

ORIENTS = 8
STEP = 0.5
PHASE = 0.1
BLOCK = 8


def tables(length):
    index = np.arange(length)
    angle = 2.0 * np.pi * ((index[:, None] * index[None, :]) % length) / length
    cosine, sine = np.cos(angle), np.sin(angle)
    forward = np.concatenate([cosine, -sine], axis=1).astype(np.float32)
    back = (np.concatenate([cosine, -sine], axis=0) / length).astype(np.float32)
    turned = jnp.asarray(np.concatenate([forward, forward], axis=0)).astype(jnp.bfloat16)
    back = jnp.asarray(back)
    high = back.astype(jnp.bfloat16)
    low = (back - high.astype(jnp.float32)).astype(jnp.bfloat16)
    return turned, high, low


def amplitudes(defocus, tilt_limits, radius, length):
    freq = jnp.arange(length, dtype=jnp.int32)
    signed = jnp.where(freq < length // 2, freq, freq - length)
    half = length // 2
    along_s = math.pi * defocus[:, None] * ((signed * signed).astype(jnp.float32) / float(half * half))[None, :] + PHASE
    along_r = math.pi * defocus[:, None] * ((radius * radius).astype(jnp.float32) / float(half * half))[None, :]
    ctf = -(
        jnp.sin(along_s)[:, None, :] * jnp.cos(along_r)[:, :, None]
        + jnp.cos(along_s)[:, None, :] * jnp.sin(along_r)[:, :, None]
    )
    limit = jnp.where(signed[None, :] >= 0, tilt_limits[:, 0][:, None], tilt_limits[:, 1][:, None])
    keep = 8 * jnp.abs(signed)[None, None, :] <= limit[:, None, :] * radius[None, :, None]
    return jnp.where(keep, ctf, 0.0)


def main_kernel(cls_ref, ori_ref, x_ref, a_ref, vol_ref, fwd_ref, high_ref, low_ref, g_ref, sc_ref, v_ref, acc_ref):
    step = pl.program_id(0)
    block, rows, length = x_ref.shape
    classes = vol_ref.shape[0]
    period = a_ref.shape[1]
    unit = ORIENTS and length // ORIENTS

    @pl.when(step == 0)
    def _():
        @pl.loop(0, classes)
        def _(k):
            spectrum = jnp.dot(vol_ref[k], fwd_ref[0:length, :], preferred_element_type=jnp.float32)
            v_ref[k] = spectrum.astype(jnp.bfloat16).astype(jnp.float32)
            acc_ref[k] = jnp.zeros(acc_ref.shape[1:], jnp.float32)

    for i in range(block):
        p = step * block + i
        k = cls_ref[p]
        start = pl.multiple_of(length - unit * ori_ref[p], unit)
        y = jnp.dot(x_ref[i], fwd_ref[pl.ds(start, length), :], preferred_element_type=jnp.float32)
        total = jnp.zeros((8, length), jnp.float32)
        for r in range(0, period, 8):
            a = a_ref[i, r : r + 8, :]
            for j in range(r, rows, period):
                for c in (0, length):
                    d = y[j : j + 8, c : c + length] - a * v_ref[k, j : j + 8, c : c + length]
                    total = total + d * d
                    acc_ref[k, j : j + 8, c : c + length] += a * d
        sc_ref[i, :] = jnp.sum(total, axis=0)

    @pl.when(step == pl.num_programs(0) - 1)
    def _():
        @pl.loop(0, classes)
        def _(k):
            s = acc_ref[k]
            s_high = s.astype(jnp.bfloat16)
            s_low = (s - s_high.astype(jnp.float32)).astype(jnp.bfloat16)
            g = jnp.dot(s_high, high_ref[...], preferred_element_type=jnp.float32)
            g += jnp.dot(s_low, high_ref[...], preferred_element_type=jnp.float32)
            g += jnp.dot(s_high, low_ref[...], preferred_element_type=jnp.float32)
            g_ref[k] = g.astype(jnp.bfloat16)


def main_call(x, a, vol, assignment, orientation, fwd, high, low):
    total, rows, length = x.shape
    classes = vol.shape[0]
    period = a.shape[1]
    whole = lambda *shape: pl.BlockSpec(shape, lambda i, *_: (0,) * len(shape))
    return pl.pallas_call(
        main_kernel,
        out_shape=(
            jax.ShapeDtypeStruct((classes, rows, length), jnp.bfloat16),
            jax.ShapeDtypeStruct((total, length), jnp.float32),
        ),
        grid_spec=pltpu.PrefetchScalarGridSpec(
            num_scalar_prefetch=2,
            grid=(total // BLOCK,),
            in_specs=[
                pl.BlockSpec((BLOCK, rows, length), lambda i, *_: (i, 0, 0)),
                pl.BlockSpec((BLOCK, period, length), lambda i, *_: (i, 0, 0)),
                whole(classes, rows, length),
                whole(2 * length, 2 * length),
                whole(2 * length, length),
                whole(2 * length, length),
            ],
            out_specs=[
                whole(classes, rows, length),
                pl.BlockSpec((BLOCK, length), lambda i, *_: (i, 0)),
            ],
            scratch_shapes=[
                pltpu.VMEM((classes, rows, 2 * length), jnp.float32),
                pltpu.VMEM((classes, rows, 2 * length), jnp.float32),
            ],
        ),
        compiler_params=pltpu.CompilerParams(vmem_limit_bytes=48 << 20),
        name="main",
    )(assignment, orientation, x, a, vol, fwd, high, low)


def local(particles, volumes, assignment, defocus, tilt_limits, orientation):
    total, rows, length = particles.shape
    fwd, high, low = tables(length)
    vol = lax.all_gather(volumes, "batch", axis=0, tiled=True)
    classes = vol.shape[0]
    period = length // 2
    first = lax.axis_index("cls") * rows
    radius = 1 + (first + jnp.arange(period, dtype=jnp.int32)) % period
    a = amplitudes(defocus, tilt_limits, radius, length)
    g, partial = main_call(particles, a, vol, assignment, orientation, fwd, high, low)
    scale = 1.0 / (rows * lax.axis_size("cls") * length * length)
    scores = lax.psum(jnp.sum(partial, axis=1) * scale, "cls")
    ids = jnp.arange(classes, dtype=jnp.int32)
    counts = jnp.sum((assignment[:, None] == ids[None, :]).astype(jnp.float32), axis=0)
    counts = lax.psum(counts, "batch")
    per = volumes.shape[0]
    mine = lax.dynamic_slice_in_dim(counts, lax.axis_index("batch") * per, per)
    grad = lax.psum_scatter(g, "batch", scatter_dimension=0, tiled=True).astype(jnp.float32)
    updated = volumes.astype(jnp.float32) + STEP * grad / (mine + 1.0)[:, None, None]
    return updated, scores


def solution(mesh):
    in_specs = (
        P("batch", "cls", None),
        P("batch", "cls", None),
        P("batch"),
        P("batch"),
        P("batch", None),
        P("batch"),
    )
    out_specs = (P("batch", "cls", None), P("batch"))
    return jax.shard_map(local, mesh=mesh, in_specs=in_specs, out_specs=out_specs, check_vma=False)
```

```python
import functools
import math

import jax
import jax.numpy as jnp
import numpy as np
from jax import lax
from jax.experimental import pallas as pl
from jax.experimental.pallas import tpu as pltpu
from jax.sharding import PartitionSpec as P

ORIENTS = 8
STEP = 0.5
PHASE = 0.1
BLOCK = 8


def tables(length):
    index = np.arange(length)
    angle = 2.0 * np.pi * ((index[:, None] * index[None, :]) % length) / length
    cosine, sine = np.cos(angle), np.sin(angle)
    forward = np.concatenate([cosine, -sine], axis=1).astype(np.float32)
    back = (np.concatenate([cosine, -sine], axis=0) / length).astype(np.float32)
    turned = jnp.asarray(np.concatenate([forward, forward], axis=0)).astype(jnp.bfloat16)
    back = jnp.asarray(back)
    high = back.astype(jnp.bfloat16)
    low = (back - high.astype(jnp.float32)).astype(jnp.bfloat16)
    return turned, high, low


MESH = pl.DeviceIdType.MESH


def sine_terms(count):
    u = np.cos(np.pi * (np.arange(4000) + 0.5) / 4000) * 0.5
    u = u[np.abs(u) > 1e-6]
    basis = np.stack([u ** (2 * i + 1) for i in range(count)], axis=1)
    return [float(c) for c in np.linalg.lstsq(basis, -np.sin(2 * np.pi * u), rcond=None)[0]]


def gather_kernel(
    defocus_ref, tilt_ref, vol_ref, counts_ref, fwd_ref, v_out, a_out, counts_out,
    buf, v_buf, a_buf, own_sem, v_sem, a_sem, ring_send, ring_recv, pair_send, pair_recv,
):
    devices, _, length = buf.shape
    rows = vol_ref.shape[1]
    total, period, _ = a_buf.shape
    depth = devices // 2
    far = depth // 2
    me = lax.axis_index("batch")
    z, core = me // 2, me % 2
    other = 1 - core
    right = ((z + 1) % depth) * 2 + core
    left = ((z + depth - 1) % depth) * 2 + core
    partner = z * 2 + other
    spans = ((0, rows // 2), (rows // 2, buf.shape[1] - rows // 2))

    own = (
        pltpu.make_async_copy(vol_ref.at[0], buf.at[me, pl.ds(0, rows)], own_sem.at[0]),
        pltpu.make_async_copy(counts_ref, buf.at[me, pl.ds(rows, counts_ref.shape[0])], own_sem.at[1]),
    )
    for copy in own:
        copy.start()
    barrier = pltpu.get_barrier_semaphore()
    for peer in (left, right, partner):
        pl.semaphore_signal(barrier, inc=1, device_id={"batch": peer}, device_id_type=MESH)
    pl.semaphore_wait(barrier, 3)
    for copy in own:
        copy.wait()

    def halves(way, s):
        return (0, 1) if s < far else ((0,) if way == 0 else (1,))

    def owner(way, s):
        return (z + depth - s) % depth if way == 0 else (z + s) % depth

    def unit(way, s, h):
        return way * 2 * far + (s - 1) * 2 + h

    def ring(way, s, h):
        at = buf.at[owner(way, s - 1) * 2 + core, pl.ds(*spans[h])]
        i = unit(way, s, h)
        return pltpu.make_async_remote_copy(
            src_ref=at, dst_ref=at, send_sem=ring_send.at[i], recv_sem=ring_recv.at[i],
            device_id={"batch": right if way == 0 else left}, device_id_type=MESH,
        )

    def arrival(way, s, h):
        at = buf.at[owner(way, s) * 2 + core, pl.ds(*spans[h])]
        i = unit(way, s, h)
        return pltpu.make_async_remote_copy(
            src_ref=at, dst_ref=at, send_sem=ring_send.at[i], recv_sem=ring_recv.at[i],
            device_id={"batch": right if way == 0 else left}, device_id_type=MESH,
        )

    def pair(zz, i, h, which):
        at = buf.at[zz * 2 + which, pl.ds(*spans[h])]
        return pltpu.make_async_remote_copy(
            src_ref=at, dst_ref=at, send_sem=pair_send.at[i], recv_sem=pair_recv.at[i],
            device_id={"batch": partner}, device_id_type=MESH,
        )

    sent = []
    own_unit = 4 * far
    for h in (0, 1):
        for way in (0, 1):
            if h in halves(way, 1):
                sent.append(ring(way, 1, h))
                sent[-1].start()
    for h in (0, 1):
        sent.append(pair(z, own_unit + h, h, core))
        sent[-1].start()

    freq = lax.broadcasted_iota(jnp.int32, (8, length), 1)
    signed = jnp.where(freq < length // 2, freq, freq - length)
    reach = (8 * jnp.abs(signed)).astype(jnp.float32)
    squares = (signed * signed).astype(jnp.float32)
    row = lax.broadcasted_iota(jnp.int32, (8, length), 0)
    radii = [(row + (1 + r)).astype(jnp.float32) for r in range(0, period, 8)]
    half = length // 2
    grid = [(squares + r * r) * (0.5 / (half * half)) for r in radii]
    terms = sine_terms(8)
    share = total // (far + 1)
    parts = [(q * share, share if q < far else total - far * share) for q in range(far + 1)]
    a_copies = []

    def filters(q):
        first, number = parts[q]

        def body(i, carry):
            p = first + i
            d = defocus_ref[p]
            limit = jnp.where(freq < length // 2, tilt_ref[2 * p], tilt_ref[2 * p + 1]).astype(jnp.float32)
            for n in range(period // 8):
                turns = d * grid[n] + PHASE / (2.0 * math.pi)
                u = turns - jnp.floor(turns + 0.5)
                w = u * u
                s = jnp.full_like(w, terms[-1])
                for c in terms[-2::-1]:
                    s = s * w + c
                a_buf[p, 8 * n : 8 * n + 8, :] = jnp.where(reach <= limit * radii[n], s * u, 0.0)
            return carry

        lax.fori_loop(0, number, body, 0)
        copy = pltpu.make_async_copy(a_buf.at[pl.ds(first, number)], a_out.at[pl.ds(first, number)], a_sem.at[q])
        copy.start()
        a_copies.append(copy)

    v_copies = []

    def transform(slot, i):
        spectrum = jnp.dot(buf[slot, 0:rows, :], fwd_ref[0:length, :], preferred_element_type=jnp.float32)
        v_buf[slot] = spectrum.astype(jnp.bfloat16)
        copy = pltpu.make_async_copy(v_buf.at[slot], v_out.at[slot], v_sem.at[i])
        copy.start()
        v_copies.append(copy)

    def from_pair(s):
        if s == 0:
            for h in (0, 1):
                pair(z, own_unit + h, h, other).wait_recv()
            transform(partner, len(v_copies))
            return
        for way in (0, 1):
            for h in halves(way, s):
                pair(owner(way, s), unit(way, s, h), h, other).wait_recv()
        for way in (0, 1) if s < far else (0,):
            transform(owner(way, s) * 2 + other, len(v_copies))

    filters(0)
    transform(me, 0)
    for s in range(1, far + 1):
        for h in (0, 1):
            for way in (0, 1):
                if h not in halves(way, s):
                    continue
                arrival(way, s, h).wait_recv()
                if s < far and h in halves(way, s + 1):
                    sent.append(ring(way, s + 1, h))
                    sent[-1].start()
                sent.append(pair(owner(way, s), unit(way, s, h), h, core))
                sent[-1].start()
        filters(s)
        for way in (0, 1) if s < far else (0,):
            transform(owner(way, s) * 2 + core, len(v_copies))
        from_pair(s - 1)
    from_pair(far)
    tally = jnp.zeros((8, length), jnp.float32)
    for b in range(devices):
        tally += buf[b, rows : rows + 8, :].astype(jnp.float32)
    counts_out[...] = tally
    for copy in sent:
        copy.wait_send()
    for copy in v_copies + a_copies:
        copy.wait()


def gather_call(volumes, counts, defocus, tilts, fwd, devices):
    _, rows, length = volumes.shape
    total = defocus.shape[0]
    period = length // 2
    anywhere = pl.BlockSpec(memory_space=pl.ANY)
    scalars = pl.BlockSpec(memory_space=pltpu.SMEM)
    inside = pl.BlockSpec(memory_space=pltpu.VMEM)
    units = 2 * devices
    return pl.pallas_call(
        gather_kernel,
        out_shape=(
            jax.ShapeDtypeStruct((devices, rows, 2 * length), jnp.bfloat16),
            jax.ShapeDtypeStruct((total, period, length), jnp.float32),
            jax.ShapeDtypeStruct((8, length), jnp.float32),
        ),
        in_specs=[scalars, scalars, anywhere, anywhere, inside],
        out_specs=(anywhere, anywhere, inside),
        scratch_shapes=[
            pltpu.VMEM((devices, rows + counts.shape[0], length), jnp.bfloat16),
            pltpu.VMEM((devices, rows, 2 * length), jnp.bfloat16),
            pltpu.VMEM((total, period, length), jnp.float32),
            pltpu.SemaphoreType.DMA((2,)),
            pltpu.SemaphoreType.DMA((devices,)),
            pltpu.SemaphoreType.DMA((devices // 4 + 1,)),
            pltpu.SemaphoreType.DMA((units,)),
            pltpu.SemaphoreType.DMA((units,)),
            pltpu.SemaphoreType.DMA((units,)),
            pltpu.SemaphoreType.DMA((units,)),
        ],
        compiler_params=pltpu.CompilerParams(collective_id=0, has_side_effects=True, vmem_limit_bytes=40 << 20),
        name="gather",
    )(defocus, tilts, volumes, counts, fwd)


def reduce_kernel(
    side, scale, g_ref, vol_ref, sc_ref, counts_ref, new_ref, scores_ref,
    from_pair, came, going, across, down,
    pair_send, pair_recv, ring_send, ring_recv, across_send, across_recv, down_send, down_recv,
):
    devices, rows, length = g_ref.shape
    depth = devices // 2
    far = depth // 2
    me = lax.axis_index("batch")
    z, core = me // 2, me % 2
    other = 1 - core
    right = ((z + 1) % depth) * 2 + core
    left = ((z + depth - 1) % depth) * 2 + core
    partner = z * 2 + other
    c = lax.axis_index("cls")
    y, x = c // side, c % side
    in_row = [y * side + (x + d) % side for d in range(1, side)]
    in_column = [((y + d) % side) * side + x for d in range(1, side)]

    barrier = pltpu.get_barrier_semaphore()
    for peer in (left, right, partner):
        pl.semaphore_signal(barrier, inc=1, device_id={"batch": peer}, device_id_type=MESH)
    for peer in in_row + in_column:
        pl.semaphore_signal(barrier, inc=1, device_id={"cls": peer}, device_id_type=MESH)
    pl.semaphore_wait(barrier, 3 + 2 * (side - 1))

    order = [far]
    for d in range(far - 1, 0, -1):
        order += [d, depth - d]
    order.append(0)
    pairs = {}
    for i, d in enumerate(order):
        j = (z + d) % depth
        pairs[d] = pltpu.make_async_remote_copy(
            src_ref=g_ref.at[2 * j + other], dst_ref=from_pair.at[j],
            send_sem=pair_send.at[i], recv_sem=pair_recv.at[i],
            device_id={"batch": partner}, device_id_type=MESH,
        )
        pairs[d].start()

    def spread(ref, send, recv, peers, axis):
        copies = []
        for d, peer in enumerate(peers, 1):
            copies.append(pltpu.make_async_remote_copy(
                src_ref=ref.at[0], dst_ref=ref.at[d], send_sem=send.at[d - 1], recv_sem=recv.at[d - 1],
                device_id={axis: peer}, device_id_type=MESH,
            ))
            copies[-1].start()
        return copies

    across[0] = lax.dot_general(
        jnp.full((8, length), scale, jnp.float32), sc_ref[...], (((1,), (1,)), ((), ())),
        precision=lax.Precision.HIGHEST, preferred_element_type=jnp.float32,
    )
    row_copies = spread(across, across_send, across_recv, in_row, "cls")

    spans = (pl.ds(0, rows // 2), pl.ds(rows // 2, rows // 2))

    def mine(j, h):
        return g_ref[2 * j + core, spans[h], :].astype(jnp.float32) + from_pair[j, spans[h], :].astype(jnp.float32)

    def began(way, s, h):
        return s > 1 or h == way

    def ring(way, s, h):
        i = way * 2 * far + (s - 1) * 2 + h
        return pltpu.make_async_remote_copy(
            src_ref=going.at[way, s - 1, spans[h]], dst_ref=came.at[way, s - 1, spans[h]],
            send_sem=ring_send.at[i], recv_sem=ring_recv.at[i],
            device_id={"batch": right if way == 0 else left}, device_id_type=MESH,
        )

    sent = []
    column_copies = None
    for s in range(1, far + 1):
        d = far + 1 - s
        for e in {d, (depth - d) % depth}:
            pairs[e].wait_recv()
        for h in (0, 1):
            for way in (0, 1):
                if not began(way, s, h):
                    continue
                j = (z + d) % depth if way == 0 else (z + depth - d) % depth
                value = mine(j, h)
                if s > 1 and began(way, s - 1, h):
                    ring(way, s - 1, h).wait_recv()
                    value += came[way, s - 2, spans[h], :].astype(jnp.float32)
                going[way, s - 1, spans[h], :] = value.astype(jnp.bfloat16)
                sent.append(ring(way, s, h))
                sent[-1].start()
        if s == 2:
            for copy in row_copies:
                copy.wait_recv()
            down[0] = sum(across[d] for d in range(1, side)) + across[0]
            column_copies = spread(down, down_send, down_recv, in_column, "cls")

    lane = lax.broadcasted_iota(jnp.int32, (1, length), 1)
    count = jnp.sum(jnp.where(lane == me, counts_ref[0:1, :], 0.0), axis=1, keepdims=True)
    factor = STEP / (count + 1.0)
    pairs[0].wait_recv()
    for h in (0, 1):
        value = mine(z, h)
        for way in (0, 1):
            ring(way, far, h).wait_recv()
            value += came[way, far - 1, spans[h], :].astype(jnp.float32)
        new_ref[0, spans[h], :] = vol_ref[0, spans[h], :].astype(jnp.float32) + value * factor
    for copy in column_copies:
        copy.wait_recv()
    scores_ref[...] = sum(down[d] for d in range(1, side)) + down[0]
    for copy in sent + row_copies + column_copies + list(pairs.values()):
        copy.wait_send()


def reduce_call(g, volumes, partial, counts, scale, lanes):
    devices, rows, length = g.shape
    depth = devices // 2
    far = depth // 2
    side = math.isqrt(lanes)
    inside = pl.BlockSpec(memory_space=pltpu.VMEM)
    sems = lambda n: pltpu.SemaphoreType.DMA((n,))
    peers = max(side - 1, 1)
    return pl.pallas_call(
        functools.partial(reduce_kernel, side, scale),
        out_shape=(
            jax.ShapeDtypeStruct((1, rows, length), jnp.float32),
            jax.ShapeDtypeStruct((8, partial.shape[0]), jnp.float32),
        ),
        in_specs=[inside] * 4,
        out_specs=(inside, inside),
        scratch_shapes=[
            pltpu.VMEM((depth, rows, length), jnp.bfloat16),
            pltpu.VMEM((2, far, rows, length), jnp.bfloat16),
            pltpu.VMEM((2, far, rows, length), jnp.bfloat16),
            pltpu.VMEM((side, 8, partial.shape[0]), jnp.float32),
            pltpu.VMEM((side, 8, partial.shape[0]), jnp.float32),
            sems(depth), sems(depth), sems(4 * far), sems(4 * far),
            sems(peers), sems(peers), sems(peers), sems(peers),
        ],
        compiler_params=pltpu.CompilerParams(collective_id=1, has_side_effects=True, vmem_limit_bytes=24 << 20),
        name="reduce",
    )(g, volumes, partial, counts)


def main_kernel(cls_ref, ori_ref, x_ref, a_ref, spec_ref, fwd_ref, high_ref, low_ref, g_ref, sc_ref, v_ref, acc_ref):
    step = pl.program_id(0)
    block, rows, length = x_ref.shape
    classes = spec_ref.shape[0]
    period = a_ref.shape[1]
    unit = ORIENTS and length // ORIENTS

    @pl.when(step == 0)
    def _():
        @pl.loop(0, classes)
        def _(k):
            v_ref[k] = spec_ref[k].astype(jnp.float32)
            acc_ref[k] = jnp.zeros(acc_ref.shape[1:], jnp.float32)

    for i in range(block):
        p = step * block + i
        k = cls_ref[p]
        start = pl.multiple_of(length - unit * ori_ref[p], unit)
        y = jnp.dot(x_ref[i], fwd_ref[pl.ds(start, length), :], preferred_element_type=jnp.float32)
        total = jnp.zeros((8, length), jnp.float32)
        for r in range(0, period, 8):
            a = a_ref[i, r : r + 8, :]
            for j in range(r, rows, period):
                for c in (0, length):
                    d = y[j : j + 8, c : c + length] - a * v_ref[k, j : j + 8, c : c + length]
                    total = total + d * d
                    acc_ref[k, j : j + 8, c : c + length] += a * d
        sc_ref[i, :] = jnp.sum(total, axis=0)

    @pl.when(step == pl.num_programs(0) - 1)
    def _():
        @pl.loop(0, classes)
        def _(k):
            s = acc_ref[k]
            s_high = s.astype(jnp.bfloat16)
            s_low = (s - s_high.astype(jnp.float32)).astype(jnp.bfloat16)
            g = jnp.dot(s_high, high_ref[...], preferred_element_type=jnp.float32)
            g += jnp.dot(s_low, high_ref[...], preferred_element_type=jnp.float32)
            g += jnp.dot(s_high, low_ref[...], preferred_element_type=jnp.float32)
            g_ref[k] = g.astype(jnp.bfloat16)


def main_call(x, a, spectra, assignment, orientation, fwd, high, low):
    total, rows, length = x.shape
    classes = spectra.shape[0]
    period = a.shape[1]
    whole = lambda *shape: pl.BlockSpec(shape, lambda i, *_: (0,) * len(shape))
    return pl.pallas_call(
        main_kernel,
        out_shape=(
            jax.ShapeDtypeStruct((classes, rows, length), jnp.bfloat16),
            jax.ShapeDtypeStruct((total, length), jnp.float32),
        ),
        grid_spec=pltpu.PrefetchScalarGridSpec(
            num_scalar_prefetch=2,
            grid=(total // BLOCK,),
            in_specs=[
                pl.BlockSpec((BLOCK, rows, length), lambda i, *_: (i, 0, 0)),
                pl.BlockSpec((BLOCK, period, length), lambda i, *_: (i, 0, 0)),
                whole(classes, rows, 2 * length),
                whole(2 * length, 2 * length),
                whole(2 * length, length),
                whole(2 * length, length),
            ],
            out_specs=[
                whole(classes, rows, length),
                pl.BlockSpec((BLOCK, length), lambda i, *_: (i, 0)),
            ],
            scratch_shapes=[
                pltpu.VMEM((classes, rows, 2 * length), jnp.float32),
                pltpu.VMEM((classes, rows, 2 * length), jnp.float32),
            ],
        ),
        compiler_params=pltpu.CompilerParams(vmem_limit_bytes=48 << 20),
        name="main",
    )(assignment, orientation, x, a, spectra, fwd, high, low)


def local(particles, volumes, assignment, defocus, tilt_limits, orientation):
    total, rows, length = particles.shape
    devices = lax.axis_size("batch")
    lanes = lax.axis_size("cls")
    assert volumes.shape[0] == 1 and rows % (length // 2) == 0
    fwd, high, low = tables(length)
    ids = jnp.arange(length, dtype=jnp.int32)
    counts = jnp.sum((assignment[:, None] == ids[None, :]).astype(jnp.float32), axis=0)
    counts = jnp.broadcast_to(counts.astype(jnp.bfloat16)[None, :], (16, length))
    spectra, a, tally = gather_call(volumes, counts, defocus, tilt_limits.reshape(-1), fwd, devices)
    g, partial = main_call(particles, a, spectra, assignment, orientation, fwd, high, low)
    scale = 1.0 / (rows * lanes * length * length)
    updated, scores = reduce_call(g, volumes, partial, tally, scale, lanes)
    return updated, scores[0]


def solution(mesh):
    in_specs = (
        P("batch", "cls", None),
        P("batch", "cls", None),
        P("batch"),
        P("batch"),
        P("batch", None),
        P("batch"),
    )
    out_specs = (P("batch", "cls", None), P("batch"))
    return jax.shard_map(local, mesh=mesh, in_specs=in_specs, out_specs=out_specs, check_vma=False)
```

```python
import functools
import math

import jax
import jax.numpy as jnp
import numpy as np
from jax import lax
from jax.experimental import pallas as pl
from jax.experimental.pallas import tpu as pltpu
from jax.sharding import PartitionSpec as P

ORIENTS = 8
STEP = 0.5
PHASE = 0.1
BLOCK = 8


def tables(length):
    index = np.arange(length)
    angle = 2.0 * np.pi * ((index[:, None] * index[None, :]) % length) / length
    cosine, sine = np.cos(angle), np.sin(angle)
    forward = np.concatenate([cosine, -sine], axis=1).astype(np.float32)
    back = (np.concatenate([cosine, -sine], axis=0) / length).astype(np.float32)
    turned = jnp.asarray(np.concatenate([forward, forward], axis=0)).astype(jnp.bfloat16)
    back = jnp.asarray(back)
    high = back.astype(jnp.bfloat16)
    low = (back - high.astype(jnp.float32)).astype(jnp.bfloat16)
    return jnp.concatenate([turned, high, low], axis=1)


MESH = pl.DeviceIdType.MESH


def sine_terms(count):
    u = np.cos(np.pi * (np.arange(4000) + 0.5) / 4000) * 0.5
    u = u[np.abs(u) > 1e-6]
    basis = np.stack([u ** (2 * i + 1) for i in range(count)], axis=1)
    return [float(c) for c in np.linalg.lstsq(basis, -np.sin(2 * np.pi * u), rcond=None)[0]]


def gather_kernel(
    defocus_in, tilt_in, class_in, vol_ref, table_ref, v_out, a_out, counts_out,
    buf, v_buf, a_buf, tally_buf, fwd_ref, tilt_ref, defocus_ref, class_ref,
    own_sem, v_sem, a_sem, ring_send, ring_recv, pair_send, pair_recv,
):
    devices, _, length = buf.shape
    rows = vol_ref.shape[1]
    total, period, _ = a_buf.shape
    depth = devices // 2
    far = depth // 2
    me = lax.axis_index("batch")
    z, core = me // 2, me % 2
    other = 1 - core
    partner = z * 2 + other

    def at_distance(way, d):
        return (z + d) % depth if way == 0 else (z + depth - d) % depth

    own = [
        pltpu.make_async_copy(class_in, class_ref, own_sem.at[0]),
        pltpu.make_async_copy(vol_ref.at[0], buf.at[me, pl.ds(0, rows)], own_sem.at[1]),
        pltpu.make_async_copy(defocus_in, defocus_ref, own_sem.at[2]),
        pltpu.make_async_copy(tilt_in, tilt_ref, own_sem.at[3]),
        pltpu.make_async_copy(table_ref.at[pl.ds(0, length), pl.ds(0, 2 * length)], fwd_ref, own_sem.at[4]),
    ]
    for copy in own:
        copy.start()
    barrier = pltpu.get_barrier_semaphore()
    for way, d in ((0, 1), (1, 1), (0, 2), (1, 2)):
        peer = at_distance(way, d) * 2 + core
        pl.semaphore_signal(barrier, inc=1, device_id={"batch": peer}, device_id_type=MESH)
    pl.semaphore_signal(barrier, inc=1, device_id={"batch": partner}, device_id_type=MESH)
    ids = lax.broadcasted_iota(jnp.int32, tally_buf.shape, 1)

    def count(p, tally):
        return tally + jnp.where(ids == class_ref[p], 1.0, 0.0)

    own[0].wait()
    tally = lax.fori_loop(0, total, count, jnp.zeros(ids.shape, jnp.float32), unroll=8)
    tally_buf[...] = tally.astype(jnp.bfloat16)
    own.append(pltpu.make_async_copy(tally_buf, buf.at[me, pl.ds(rows, tally_buf.shape[0])], own_sem.at[5]))
    own[-1].start()
    for copy in own[1:]:
        copy.wait()
    pl.semaphore_wait(barrier, 5)

    spans = (pl.ds(0, rows // 2), pl.ds(rows // 2, buf.shape[1] - rows // 2))

    def halves(way, d):
        return (0, 1) if d < far else (way,)

    def unit(way, d, h):
        return (way * far + d - 1) * 2 + h

    def ring(way, d, h, first):
        at = buf.at[at_distance(1 - way, first) * 2 + core, spans[h]]
        i = unit(way, d, h)
        return pltpu.make_async_remote_copy(
            src_ref=at, dst_ref=at, send_sem=ring_send.at[i], recv_sem=ring_recv.at[i],
            device_id={"batch": at_distance(way, d - first) * 2 + core}, device_id_type=MESH,
        )

    def arrival(way, d, h):
        at = buf.at[at_distance(1 - way, d) * 2 + core, spans[h]]
        i = unit(way, d, h)
        return pltpu.make_async_remote_copy(
            src_ref=at, dst_ref=at, send_sem=ring_send.at[i], recv_sem=ring_recv.at[i],
            device_id={"batch": at_distance(way, 1) * 2 + core}, device_id_type=MESH,
        )

    def pair(zz, i, h, which):
        at = buf.at[zz * 2 + which, spans[h]]
        return pltpu.make_async_remote_copy(
            src_ref=at, dst_ref=at, send_sem=pair_send.at[i], recv_sem=pair_recv.at[i],
            device_id={"batch": partner}, device_id_type=MESH,
        )

    sent = []
    own_unit = 4 * far

    def send(copy):
        copy.start()
        sent.append(copy)

    for d in (2, 1):
        for h in (0, 1):
            for way in (0, 1):
                send(ring(way, d, h, 0))
    for h in (0, 1):
        send(pair(z, own_unit + h, h, core))

    freq = lax.broadcasted_iota(jnp.int32, (8, length), 1)
    row = lax.broadcasted_iota(jnp.int32, (8, length), 0)
    signed = jnp.where(freq < length // 2, freq, freq - length)
    reach = (8 * jnp.abs(signed)).astype(jnp.float32)
    half = length // 2
    along_s = (signed * signed).astype(jnp.float32) * (0.5 / (half * half))
    lane_radius = 8 * (freq % 8) + row + 1
    along_r = (lane_radius * lane_radius).astype(jnp.float32) * (0.5 / (half * half))
    radii = [(row + (1 + r)).astype(jnp.float32) for r in range(0, period, 8)]
    phase = PHASE / (2.0 * math.pi)
    terms = sine_terms(7)

    def minus_sine(turns):
        u = turns - jnp.floor(turns + 0.5)
        w = u * u
        s = jnp.full_like(w, terms[-1])
        for c in terms[-2::-1]:
            s = s * w + c
        return s * u

    group = length // 8
    groups = total // group
    bounds = [q * groups // (far + 1) for q in range(far + 2)]
    a_copies = []

    def filters(q):
        first, last = bounds[q], bounds[q + 1]

        def body(b, carry):
            base = b * group
            ds = [defocus_ref[base + i] for i in range(group)]
            by_lane = jnp.full((8, length), ds[0], jnp.float32)
            for i in range(1, group):
                by_lane = jnp.where(freq >= 8 * i, ds[i], by_lane)
            turns_r = by_lane * along_r
            sine_r = minus_sine(turns_r)
            cosine_r = minus_sine(turns_r + 0.25)
            for e in range(0, group, 8):
                by_row = jnp.full((8, length), ds[e], jnp.float32)
                for i in range(1, 8):
                    by_row = jnp.where(row >= i, ds[e + i], by_row)
                turns_s = by_row * along_s + phase
                sine_s = minus_sine(turns_s)
                cosine_s = minus_sine(turns_s + 0.25)
                for i in range(8):
                    at = 8 * (e + i)
                    ss = jnp.broadcast_to(sine_s[i : i + 1, :], (8, length))
                    cs = jnp.broadcast_to(cosine_s[i : i + 1, :], (8, length))
                    tilt = tilt_ref[pl.ds(base + e + i, 1), :].astype(jnp.float32)
                    plus = jnp.broadcast_to(tilt[:, 0:1], (8, length))
                    limit = jnp.where(freq < length // 2, plus, jnp.broadcast_to(tilt[:, 1:2], (8, length)))
                    for n in range(period // 8):
                        sr = jnp.broadcast_to(sine_r[:, at + n : at + n + 1], (8, length))
                        cr = jnp.broadcast_to(cosine_r[:, at + n : at + n + 1], (8, length))
                        keep = reach <= limit * radii[n]
                        a_buf[base + e + i, 8 * n : 8 * n + 8, :] = jnp.where(keep, -(ss * cr + cs * sr), 0.0)
            return carry

        lax.fori_loop(first, last, body, 0)
        at = pl.ds(first * group, (last - first) * group)
        if last > first:
            a_copies.append(pltpu.make_async_copy(a_buf.at[at], a_out.at[at], a_sem.at[q]))
            a_copies[-1].start()

    v_copies = []

    def transform(slot, i):
        spectrum = jnp.dot(buf[slot, 0:rows, :], fwd_ref[0:length, :], preferred_element_type=jnp.float32)
        v_buf[slot] = spectrum.astype(jnp.bfloat16)
        copy = pltpu.make_async_copy(v_buf.at[slot], v_out.at[slot], v_sem.at[i])
        copy.start()
        v_copies.append(copy)

    def arrived(d):
        for h in (0, 1):
            for way in (0, 1):
                if h not in halves(way, d):
                    continue
                arrival(way, d, h).wait_recv()
                if d == 2:
                    send(ring(way, 3, h, 2))
                    if h in halves(way, far):
                        send(ring(way, far, h, 2))
        for h in (0, 1):
            for way in (0, 1):
                if h in halves(way, d):
                    send(pair(at_distance(1 - way, d), unit(way, d, h), h, core))

    def transforms(d):
        if d == 0:
            for h in (0, 1):
                pair(z, own_unit + h, h, other).wait_recv()
            transform(partner, len(v_copies))
            return
        for way in (0, 1) if d < far else (0,):
            transform(at_distance(1 - way, d) * 2 + core, len(v_copies))
        for way in (0, 1):
            for h in halves(way, d):
                pair(at_distance(1 - way, d), unit(way, d, h), h, other).wait_recv()
        for way in (0, 1) if d < far else (0,):
            transform(at_distance(1 - way, d) * 2 + other, len(v_copies))

    transform(me, 0)
    filters(0)
    arrived(2)
    filters(1)
    arrived(1)
    filters(2)
    transforms(0)
    transforms(2)
    transforms(1)
    arrived(3)
    filters(3)
    arrived(far)
    filters(4)
    transforms(3)
    transforms(far)
    tally = jnp.zeros((8, length), jnp.float32)
    for b in range(devices):
        tally += buf[b, rows : rows + 8, :].astype(jnp.float32)
    counts_out[...] = tally
    for copy in sent:
        copy.wait_send()
    for copy in v_copies + a_copies:
        copy.wait()


def gather_call(volumes, assignment, defocus, tilts, table, devices):
    _, rows, length = volumes.shape
    total = defocus.shape[0]
    period = length // 2
    assert devices == 16
    anywhere = pl.BlockSpec(memory_space=pl.ANY)
    inside = pl.BlockSpec(memory_space=pltpu.VMEM)
    sems = lambda n: pltpu.SemaphoreType.DMA((n,))
    return pl.pallas_call(
        gather_kernel,
        out_shape=(
            jax.ShapeDtypeStruct((devices, rows, 2 * length), jnp.bfloat16),
            jax.ShapeDtypeStruct((total, period, length), jnp.float32),
            jax.ShapeDtypeStruct((8, length), jnp.float32),
        ),
        in_specs=[pl.BlockSpec(memory_space=pltpu.HBM)] * 5,
        out_specs=(anywhere, anywhere, inside),
        scratch_shapes=[
            pltpu.VMEM((devices, rows + 16, length), jnp.bfloat16),
            pltpu.VMEM((devices, rows, 2 * length), jnp.bfloat16),
            pltpu.VMEM((total, period, length), jnp.float32),
            pltpu.VMEM((16, length), jnp.bfloat16),
            pltpu.VMEM((length, 2 * length), jnp.bfloat16),
            pltpu.VMEM(tilts.shape, jnp.int32),
            pltpu.SMEM((total,), jnp.float32),
            pltpu.SMEM((total,), jnp.int32),
            sems(6), sems(devices), sems(5),
            sems(devices), sems(devices), sems(devices + 2), sems(devices + 2),
        ],
        compiler_params=pltpu.CompilerParams(collective_id=0, has_side_effects=True, vmem_limit_bytes=16 << 20),
        name="gather",
    )(defocus, tilts, assignment, volumes, table)


def reduce_kernel(
    side, scale, g_ref, vol_ref, sc_ref, counts_ref, new_ref, scores_ref,
    from_pair, came, going, across, down,
    pair_send, pair_recv, ring_send, ring_recv, across_send, across_recv, down_send, down_recv,
):
    devices, rows, length = g_ref.shape
    depth = devices // 2
    far = depth // 2
    me = lax.axis_index("batch")
    z, core = me // 2, me % 2
    other = 1 - core
    partner = z * 2 + other
    c = lax.axis_index("cls")
    y, x = c // side, c % side
    in_row = [y * side + (x + d) % side for d in range(1, side)]
    in_column = [((y + d) % side) * side + x for d in range(1, side)]

    def at_distance(way, d):
        return (z + d) % depth if way == 0 else (z + depth - d) % depth

    barrier = pltpu.get_barrier_semaphore()
    for way, d in ((0, 1), (1, 1), (0, 2), (1, 2)):
        peer = at_distance(way, d) * 2 + core
        pl.semaphore_signal(barrier, inc=1, device_id={"batch": peer}, device_id_type=MESH)
    pl.semaphore_signal(barrier, inc=1, device_id={"batch": partner}, device_id_type=MESH)
    for peer in in_row + in_column:
        pl.semaphore_signal(barrier, inc=1, device_id={"cls": peer}, device_id_type=MESH)
    pl.semaphore_wait(barrier, 5 + 2 * (side - 1))

    order = [far]
    for d in range(far - 1, 0, -1):
        order += [d, depth - d]
    order.append(0)
    pairs = {}
    for i, d in enumerate(order):
        j = (z + d) % depth
        pairs[d] = pltpu.make_async_remote_copy(
            src_ref=g_ref.at[2 * j + other], dst_ref=from_pair.at[j],
            send_sem=pair_send.at[i], recv_sem=pair_recv.at[i],
            device_id={"batch": partner}, device_id_type=MESH,
        )
        pairs[d].start()

    def spread(ref, send, recv, peers, axis):
        copies = []
        for d, peer in enumerate(peers, 1):
            copies.append(pltpu.make_async_remote_copy(
                src_ref=ref.at[0], dst_ref=ref.at[d], send_sem=send.at[d - 1], recv_sem=recv.at[d - 1],
                device_id={axis: peer}, device_id_type=MESH,
            ))
            copies[-1].start()
        return copies

    across[0] = lax.dot_general(
        jnp.full((8, length), scale, jnp.float32), sc_ref[...], (((1,), (1,)), ((), ())),
        precision=lax.Precision.HIGHEST, preferred_element_type=jnp.float32,
    )
    row_copies = spread(across, across_send, across_recv, in_row, "cls")

    spans = (pl.ds(0, rows // 2), pl.ds(rows // 2, rows // 2))

    def mine(j, h):
        return g_ref[2 * j + core, spans[h], :].astype(jnp.float32) + from_pair[j, spans[h], :].astype(jnp.float32)

    def ring(way, d, h):
        i = (way * far + d - 1) * 2 + h
        return pltpu.make_async_remote_copy(
            src_ref=going.at[way, d - 1, spans[h]], dst_ref=came.at[way, d - 1, spans[h]],
            send_sem=ring_send.at[i], recv_sem=ring_recv.at[i],
            device_id={"batch": at_distance(way, d if d < 3 else d - 2) * 2 + core}, device_id_type=MESH,
        )

    sent = []

    def send(way, d, h, value):
        going[way, d - 1, spans[h], :] = value.astype(jnp.bfloat16)
        sent.append(ring(way, d, h))
        sent[-1].start()

    def landed(way, d, h):
        ring(way, d, h).wait_recv()
        return came[way, d - 1, spans[h], :].astype(jnp.float32)

    pairs[far].wait_recv()
    for way in (0, 1):
        send(way, far, way, mine(at_distance(way, far), way))
    for d in (3, 1):
        if d == 1:
            for copy in row_copies:
                copy.wait_recv()
            down[0] = sum(across[d] for d in range(1, side)) + across[0]
            column_copies = spread(down, down_send, down_recv, in_column, "cls")
        for way in (0, 1):
            pairs[d if way == 0 else depth - d].wait_recv()
            for h in (0, 1):
                send(way, d, h, mine(at_distance(way, d), h))
        if d == 3:
            for way in (0, 1):
                pairs[2 if way == 0 else depth - 2].wait_recv()
    for h in (0, 1):
        for way in (0, 1):
            value = mine(at_distance(way, 2), h) + landed(way, 3, h)
            if h == way:
                value += landed(way, far, h)
            send(way, 2, h, value)

    lane = lax.broadcasted_iota(jnp.int32, (1, length), 1)
    count = jnp.sum(jnp.where(lane == me, counts_ref[0:1, :], 0.0), axis=1, keepdims=True)
    factor = STEP / (count + 1.0)
    pairs[0].wait_recv()
    for h in (0, 1):
        value = mine(z, h)
        for d in (1, 2):
            for way in (0, 1):
                value += landed(way, d, h)
        new_ref[0, spans[h], :] = vol_ref[0, spans[h], :].astype(jnp.float32) + value * factor
    for copy in column_copies:
        copy.wait_recv()
    scores_ref[...] = sum(down[d] for d in range(1, side)) + down[0]
    for copy in sent + row_copies + column_copies + list(pairs.values()):
        copy.wait_send()


def reduce_call(g, volumes, partial, counts, scale, lanes):
    devices, rows, length = g.shape
    depth = devices // 2
    far = depth // 2
    side = math.isqrt(lanes)
    inside = pl.BlockSpec(memory_space=pltpu.VMEM)
    sems = lambda n: pltpu.SemaphoreType.DMA((n,))
    peers = max(side - 1, 1)
    return pl.pallas_call(
        functools.partial(reduce_kernel, side, scale),
        out_shape=(
            jax.ShapeDtypeStruct((1, rows, length), jnp.float32),
            jax.ShapeDtypeStruct((8, partial.shape[0]), jnp.float32),
        ),
        in_specs=[inside] * 4,
        out_specs=(inside, inside),
        scratch_shapes=[
            pltpu.VMEM((depth, rows, length), jnp.bfloat16),
            pltpu.VMEM((2, far, rows, length), jnp.bfloat16),
            pltpu.VMEM((2, far, rows, length), jnp.bfloat16),
            pltpu.VMEM((side, 8, partial.shape[0]), jnp.float32),
            pltpu.VMEM((side, 8, partial.shape[0]), jnp.float32),
            sems(depth), sems(depth), sems(4 * far), sems(4 * far),
            sems(peers), sems(peers), sems(peers), sems(peers),
        ],
        compiler_params=pltpu.CompilerParams(collective_id=1, has_side_effects=True, vmem_limit_bytes=12 << 20),
        name="reduce",
    )(g, volumes, partial, counts)


def main_kernel(
    x_ref, a_ref, spec_ref, table_ref, class_in, orient_in, g_ref, sc_ref,
    v_ref, acc_ref, fwd_ref, high_ref, low_ref, cls_ref, ori_ref, sem,
):
    step = pl.program_id(0)
    block, rows, length = x_ref.shape
    classes = spec_ref.shape[0]
    period = a_ref.shape[1]
    unit = length // ORIENTS

    @pl.when(step == 0)
    def _():
        copies = [
            pltpu.make_async_copy(table_ref.at[:, pl.ds(0, 2 * length)], fwd_ref, sem.at[0]),
            pltpu.make_async_copy(table_ref.at[:, pl.ds(2 * length, length)], high_ref, sem.at[1]),
            pltpu.make_async_copy(table_ref.at[:, pl.ds(3 * length, length)], low_ref, sem.at[2]),
            pltpu.make_async_copy(class_in, cls_ref, sem.at[3]),
            pltpu.make_async_copy(orient_in, ori_ref, sem.at[4]),
        ]
        for copy in copies:
            copy.start()

        @pl.loop(0, classes)
        def _(k):
            v_ref[k] = spec_ref[k].astype(jnp.float32)
            acc_ref[k] = jnp.zeros(acc_ref.shape[1:], jnp.float32)

        for copy in copies:
            copy.wait()

    for i in range(block):
        p = step * block + i
        k = cls_ref[p]
        start = pl.multiple_of(length - unit * ori_ref[p], unit)
        y = jnp.dot(x_ref[i], fwd_ref[pl.ds(start, length), :], preferred_element_type=jnp.float32)
        total = jnp.zeros((8, length), jnp.float32)
        for r in range(0, period, 8):
            a = a_ref[i, r : r + 8, :]
            for j in range(r, rows, period):
                for c in (0, length):
                    d = y[j : j + 8, c : c + length] - a * v_ref[k, j : j + 8, c : c + length]
                    total = total + d * d
                    acc_ref[k, j : j + 8, c : c + length] += a * d
        sc_ref[i, :] = jnp.sum(total, axis=0)

    @pl.when(step == pl.num_programs(0) - 1)
    def _():
        @pl.loop(0, classes)
        def _(k):
            s = acc_ref[k]
            s_high = s.astype(jnp.bfloat16)
            s_low = (s - s_high.astype(jnp.float32)).astype(jnp.bfloat16)
            g = jnp.dot(s_high, high_ref[...], preferred_element_type=jnp.float32)
            g += jnp.dot(s_low, high_ref[...], preferred_element_type=jnp.float32)
            g += jnp.dot(s_high, low_ref[...], preferred_element_type=jnp.float32)
            g_ref[k] = g.astype(jnp.bfloat16)


def main_call(x, a, spectra, assignment, orientation, table):
    total, rows, length = x.shape
    classes = spectra.shape[0]
    period = a.shape[1]
    outside = pl.BlockSpec(memory_space=pltpu.HBM)
    return pl.pallas_call(
        main_kernel,
        out_shape=(
            jax.ShapeDtypeStruct((classes, rows, length), jnp.bfloat16),
            jax.ShapeDtypeStruct((total, length), jnp.float32),
        ),
        grid=(total // BLOCK,),
        in_specs=[
            pl.BlockSpec((BLOCK, rows, length), lambda i: (i, 0, 0)),
            pl.BlockSpec((BLOCK, period, length), lambda i: (i, 0, 0)),
            pl.BlockSpec((classes, rows, 2 * length), lambda i: (0, 0, 0)),
            outside, outside, outside,
        ],
        out_specs=[
            pl.BlockSpec((classes, rows, length), lambda i: (0, 0, 0)),
            pl.BlockSpec((BLOCK, length), lambda i: (i, 0)),
        ],
        scratch_shapes=[
            pltpu.VMEM((classes, rows, 2 * length), jnp.float32),
            pltpu.VMEM((classes, rows, 2 * length), jnp.float32),
            pltpu.VMEM((2 * length, 2 * length), jnp.bfloat16),
            pltpu.VMEM((2 * length, length), jnp.bfloat16),
            pltpu.VMEM((2 * length, length), jnp.bfloat16),
            pltpu.SMEM((total,), jnp.int32),
            pltpu.SMEM((total,), jnp.int32),
            pltpu.SemaphoreType.DMA((5,)),
        ],
        compiler_params=pltpu.CompilerParams(vmem_limit_bytes=44 << 20),
        name="main",
    )(x, a, spectra, table, assignment, orientation)


def local(particles, volumes, assignment, defocus, tilt_limits, orientation):
    total, rows, length = particles.shape
    devices = lax.axis_size("batch")
    lanes = lax.axis_size("cls")
    assert volumes.shape[0] == 1 and rows % (length // 2) == 0
    table = tables(length)
    hbm = lambda v: pltpu.with_memory_space_constraint(v, pltpu.HBM)
    volumes, assignment, defocus, tilt_limits, table, orientation, particles = map(
        hbm, (volumes, assignment, defocus, tilt_limits, table, orientation, particles)
    )
    spectra, a, tally = gather_call(volumes, assignment, defocus, tilt_limits, table, devices)
    g, partial = main_call(particles, a, spectra, assignment, orientation, table)
    scale = 1.0 / (rows * lanes * length * length)
    updated, scores = reduce_call(g, volumes, partial, tally, scale, lanes)
    return updated, scores[0]


def solution(mesh):
    in_specs = (
        P("batch", "cls", None),
        P("batch", "cls", None),
        P("batch"),
        P("batch"),
        P("batch", None),
        P("batch"),
    )
    out_specs = (P("batch", "cls", None), P("batch"))
    return jax.shard_map(local, mesh=mesh, in_specs=in_specs, out_specs=out_specs, check_vma=False)
```

```python
import functools
import math

import jax
import jax.numpy as jnp
import numpy as np
from jax import lax
from jax.experimental import pallas as pl
from jax.experimental.pallas import tpu as pltpu
from jax.sharding import PartitionSpec as P

ORIENTS = 8
STEP = 0.5
PHASE = 0.1
BLOCK = 16


def tables(length):
    index = np.arange(length)
    angle = 2.0 * np.pi * ((index[:, None] * index[None, :]) % length) / length
    cosine, sine = np.cos(angle), np.sin(angle)
    forward = np.concatenate([cosine, -sine], axis=1).astype(np.float32)
    back = (np.concatenate([cosine, -sine], axis=0) / length).astype(np.float32)
    turned = jnp.asarray(np.concatenate([forward, forward], axis=0)).astype(jnp.bfloat16)
    back = jnp.asarray(back)
    high = back.astype(jnp.bfloat16)
    low = (back - high.astype(jnp.float32)).astype(jnp.bfloat16)
    return jnp.concatenate([turned, high, low], axis=1)


MESH = pl.DeviceIdType.MESH


def sine_terms(count):
    u = np.cos(np.pi * (np.arange(4000) + 0.5) / 4000) * 0.5
    u = u[np.abs(u) > 1e-6]
    basis = np.stack([u ** (2 * i + 1) for i in range(count)], axis=1)
    return [float(c) for c in np.linalg.lstsq(basis, -np.sin(2 * np.pi * u), rcond=None)[0]]


def gather_kernel(
    defocus_in, tilt_in, class_in, vol_ref, table_ref, v_out, a_out, counts_out,
    buf, v_buf, a_buf, tally_buf, fwd_ref, tilt_ref, defocus_ref, class_ref,
    own_sem, v_sem, a_sem, ring_send, ring_recv, pair_send, pair_recv,
):
    devices, _, length = buf.shape
    rows = vol_ref.shape[1]
    total, period, _ = a_buf.shape
    depth = devices // 2
    far = depth // 2
    me = lax.axis_index("batch")
    z, core = me // 2, me % 2
    other = 1 - core
    partner = z * 2 + other

    def at_distance(way, d):
        return (z + d) % depth if way == 0 else (z + depth - d) % depth

    own = [
        pltpu.make_async_copy(class_in, class_ref, own_sem.at[0]),
        pltpu.make_async_copy(vol_ref.at[0], buf.at[me, pl.ds(0, rows)], own_sem.at[1]),
        pltpu.make_async_copy(defocus_in, defocus_ref, own_sem.at[2]),
        pltpu.make_async_copy(tilt_in, tilt_ref, own_sem.at[3]),
        pltpu.make_async_copy(table_ref.at[pl.ds(0, length), pl.ds(0, 2 * length)], fwd_ref, own_sem.at[4]),
    ]
    for copy in own:
        copy.start()
    barrier = pltpu.get_barrier_semaphore()
    for way, d in ((0, 1), (1, 1), (0, 2), (1, 2)):
        peer = at_distance(way, d) * 2 + core
        pl.semaphore_signal(barrier, inc=1, device_id={"batch": peer}, device_id_type=MESH)
    pl.semaphore_signal(barrier, inc=1, device_id={"batch": partner}, device_id_type=MESH)
    ids = lax.broadcasted_iota(jnp.int32, tally_buf.shape, 1)

    def count(p, tally):
        return tally + jnp.where(ids == class_ref[p], 1.0, 0.0)

    own[0].wait()
    tally = lax.fori_loop(0, total, count, jnp.zeros(ids.shape, jnp.float32), unroll=8)
    tally_buf[...] = tally.astype(jnp.bfloat16)
    own.append(pltpu.make_async_copy(tally_buf, buf.at[me, pl.ds(rows, tally_buf.shape[0])], own_sem.at[5]))
    own[-1].start()
    for copy in own[1:]:
        copy.wait()
    freq = lax.broadcasted_iota(jnp.int32, (8, length), 1)
    row = lax.broadcasted_iota(jnp.int32, (8, length), 0)
    signed = jnp.where(freq < length // 2, freq, freq - length)
    reach = (8 * jnp.abs(signed)).astype(jnp.float32)
    half = length // 2
    along_s = (signed * signed).astype(jnp.float32) * (0.5 / (half * half))
    lane_radius = 8 * (freq % 8) + row + 1
    along_r = (lane_radius * lane_radius).astype(jnp.float32) * (0.5 / (half * half))
    radii = [(row + (1 + r)).astype(jnp.float32) for r in range(0, period, 8)]
    phase = PHASE / (2.0 * math.pi)
    terms = sine_terms(7)

    def minus_sine(turns):
        u = turns - jnp.floor(turns + 0.5)
        w = u * u
        s = jnp.full_like(w, terms[-1])
        for c in terms[-2::-1]:
            s = s * w + c
        return s * u

    group = length // 8
    groups = total // group
    bounds = [q * groups // (far + 1) for q in range(far + 2)]
    a_copies = []

    def filters(q):
        first, last = bounds[q], bounds[q + 1]

        def body(b, carry):
            base = b * group
            ds = [defocus_ref[base + i] for i in range(group)]
            by_lane = jnp.full((8, length), ds[0], jnp.float32)
            for i in range(1, group):
                by_lane = jnp.where(freq >= 8 * i, ds[i], by_lane)
            turns_r = by_lane * along_r
            sine_r = minus_sine(turns_r)
            cosine_r = minus_sine(turns_r + 0.25)
            for e in range(0, group, 8):
                by_row = jnp.full((8, length), ds[e], jnp.float32)
                for i in range(1, 8):
                    by_row = jnp.where(row >= i, ds[e + i], by_row)
                turns_s = by_row * along_s + phase
                sine_s = minus_sine(turns_s)
                cosine_s = minus_sine(turns_s + 0.25)
                for i in range(8):
                    at = 8 * (e + i)
                    ss = jnp.broadcast_to(sine_s[i : i + 1, :], (8, length))
                    cs = jnp.broadcast_to(cosine_s[i : i + 1, :], (8, length))
                    tilt = tilt_ref[pl.ds(base + e + i, 1), :].astype(jnp.float32)
                    plus = jnp.broadcast_to(tilt[:, 0:1], (8, length))
                    limit = jnp.where(freq < length // 2, plus, jnp.broadcast_to(tilt[:, 1:2], (8, length)))
                    for n in range(period // 8):
                        sr = jnp.broadcast_to(sine_r[:, at + n : at + n + 1], (8, length))
                        cr = jnp.broadcast_to(cosine_r[:, at + n : at + n + 1], (8, length))
                        keep = reach <= limit * radii[n]
                        a_buf[base + e + i, 8 * n : 8 * n + 8, :] = jnp.where(keep, -(ss * cr + cs * sr), 0.0)
            return carry

        lax.fori_loop(first, last, body, 0)
        at = pl.ds(first * group, (last - first) * group)
        if last > first:
            a_copies.append(pltpu.make_async_copy(a_buf.at[at], a_out.at[at], a_sem.at[q]))
            a_copies[-1].start()

    for q in range(far + 1):
        filters(q)
    pl.semaphore_wait(barrier, 5)

    spans = (pl.ds(0, rows // 2), pl.ds(rows // 2, buf.shape[1] - rows // 2))

    def halves(way, d):
        return (0, 1) if d < far else (way,)

    def unit(way, d, h):
        return (way * far + d - 1) * 2 + h

    def ring(way, d, h, first):
        at = buf.at[at_distance(1 - way, first) * 2 + core, spans[h]]
        i = unit(way, d, h)
        return pltpu.make_async_remote_copy(
            src_ref=at, dst_ref=at, send_sem=ring_send.at[i], recv_sem=ring_recv.at[i],
            device_id={"batch": at_distance(way, d - first) * 2 + core}, device_id_type=MESH,
        )

    def arrival(way, d, h):
        at = buf.at[at_distance(1 - way, d) * 2 + core, spans[h]]
        i = unit(way, d, h)
        return pltpu.make_async_remote_copy(
            src_ref=at, dst_ref=at, send_sem=ring_send.at[i], recv_sem=ring_recv.at[i],
            device_id={"batch": at_distance(way, 1) * 2 + core}, device_id_type=MESH,
        )

    def pair(zz, i, h, which):
        at = buf.at[zz * 2 + which, spans[h]]
        return pltpu.make_async_remote_copy(
            src_ref=at, dst_ref=at, send_sem=pair_send.at[i], recv_sem=pair_recv.at[i],
            device_id={"batch": partner}, device_id_type=MESH,
        )

    sent = []
    own_unit = 4 * far

    def send(copy):
        copy.start()
        sent.append(copy)

    for d in (2, 1):
        for h in (0, 1):
            for way in (0, 1):
                send(ring(way, d, h, 0))
    for h in (0, 1):
        send(pair(z, own_unit + h, h, core))

    v_copies = []

    def transform(slot, i):
        spectrum = jnp.dot(buf[slot, 0:rows, :], fwd_ref[0:length, :], preferred_element_type=jnp.float32)
        v_buf[slot] = spectrum.astype(jnp.bfloat16)
        copy = pltpu.make_async_copy(v_buf.at[slot], v_out.at[slot], v_sem.at[i])
        copy.start()
        v_copies.append(copy)

    def arrived(d):
        for h in (0, 1):
            for way in (0, 1):
                if h not in halves(way, d):
                    continue
                arrival(way, d, h).wait_recv()
                if d == 2:
                    send(ring(way, 3, h, 2))
                    if h in halves(way, far):
                        send(ring(way, far, h, 2))
        for h in (0, 1):
            for way in (0, 1):
                if h in halves(way, d):
                    send(pair(at_distance(1 - way, d), unit(way, d, h), h, core))

    def transforms(d):
        if d == 0:
            for h in (0, 1):
                pair(z, own_unit + h, h, other).wait_recv()
            transform(partner, len(v_copies))
            return
        for way in (0, 1) if d < far else (0,):
            transform(at_distance(1 - way, d) * 2 + core, len(v_copies))
        for way in (0, 1):
            for h in halves(way, d):
                pair(at_distance(1 - way, d), unit(way, d, h), h, other).wait_recv()
        for way in (0, 1) if d < far else (0,):
            transform(at_distance(1 - way, d) * 2 + other, len(v_copies))

    transform(me, 0)
    arrived(2)
    arrived(1)
    transforms(0)
    transforms(2)
    transforms(1)
    arrived(3)
    arrived(far)
    transforms(3)
    transforms(far)
    tally = jnp.zeros((8, length), jnp.float32)
    for b in range(devices):
        tally += buf[b, rows : rows + 8, :].astype(jnp.float32)
    counts_out[...] = tally
    for copy in sent:
        copy.wait_send()
    for copy in v_copies + a_copies:
        copy.wait()


def gather_call(volumes, assignment, defocus, tilts, table, devices):
    _, rows, length = volumes.shape
    total = defocus.shape[0]
    period = length // 2
    assert devices == 16
    anywhere = pl.BlockSpec(memory_space=pl.ANY)
    inside = pl.BlockSpec(memory_space=pltpu.VMEM)
    sems = lambda n: pltpu.SemaphoreType.DMA((n,))
    return pl.pallas_call(
        gather_kernel,
        out_shape=(
            jax.ShapeDtypeStruct((devices, rows, 2 * length), jnp.bfloat16),
            jax.ShapeDtypeStruct((total, period, length), jnp.float32),
            jax.ShapeDtypeStruct((8, length), jnp.float32),
        ),
        in_specs=[pl.BlockSpec(memory_space=pltpu.HBM)] * 5,
        out_specs=(anywhere, anywhere, inside),
        scratch_shapes=[
            pltpu.VMEM((devices, rows + 16, length), jnp.bfloat16),
            pltpu.VMEM((devices, rows, 2 * length), jnp.bfloat16),
            pltpu.VMEM((total, period, length), jnp.float32),
            pltpu.VMEM((16, length), jnp.bfloat16),
            pltpu.VMEM((length, 2 * length), jnp.bfloat16),
            pltpu.VMEM(tilts.shape, jnp.int32),
            pltpu.SMEM((total,), jnp.float32),
            pltpu.SMEM((total,), jnp.int32),
            sems(6), sems(devices), sems(5),
            sems(devices), sems(devices), sems(devices + 2), sems(devices + 2),
        ],
        compiler_params=pltpu.CompilerParams(collective_id=0, has_side_effects=True, vmem_limit_bytes=16 << 20),
        name="gather",
    )(defocus, tilts, assignment, volumes, table)


def reduce_kernel(
    side, scale, g_ref, vol_ref, sc_ref, counts_ref, new_ref, scores_ref,
    from_pair, came, going, across, down,
    pair_send, pair_recv, ring_send, ring_recv, across_send, across_recv, down_send, down_recv,
):
    devices, rows, length = g_ref.shape
    depth = devices // 2
    far = depth // 2
    me = lax.axis_index("batch")
    z, core = me // 2, me % 2
    other = 1 - core
    partner = z * 2 + other
    c = lax.axis_index("cls")
    y, x = c // side, c % side
    in_row = [y * side + (x + d) % side for d in range(1, side)]
    in_column = [((y + d) % side) * side + x for d in range(1, side)]

    def at_distance(way, d):
        return (z + d) % depth if way == 0 else (z + depth - d) % depth

    barrier = pltpu.get_barrier_semaphore()
    for way, d in ((0, 1), (1, 1), (0, 2), (1, 2)):
        peer = at_distance(way, d) * 2 + core
        pl.semaphore_signal(barrier, inc=1, device_id={"batch": peer}, device_id_type=MESH)
    pl.semaphore_signal(barrier, inc=1, device_id={"batch": partner}, device_id_type=MESH)
    for peer in in_row + in_column:
        pl.semaphore_signal(barrier, inc=1, device_id={"cls": peer}, device_id_type=MESH)
    across[0] = lax.dot_general(
        jnp.full((8, length), scale, jnp.float32), sc_ref[...], (((1,), (1,)), ((), ())),
        precision=lax.Precision.HIGHEST, preferred_element_type=jnp.float32,
    )
    pl.semaphore_wait(barrier, 5 + 2 * (side - 1))

    order = [far]
    for d in range(far - 1, 0, -1):
        order += [d, depth - d]
    order.append(0)
    pairs = {}
    for i, d in enumerate(order):
        j = (z + d) % depth
        pairs[d] = pltpu.make_async_remote_copy(
            src_ref=g_ref.at[2 * j + other], dst_ref=from_pair.at[j],
            send_sem=pair_send.at[i], recv_sem=pair_recv.at[i],
            device_id={"batch": partner}, device_id_type=MESH,
        )
        pairs[d].start()

    def spread(ref, send, recv, peers, axis):
        copies = []
        for d, peer in enumerate(peers, 1):
            copies.append(pltpu.make_async_remote_copy(
                src_ref=ref.at[0], dst_ref=ref.at[d], send_sem=send.at[d - 1], recv_sem=recv.at[d - 1],
                device_id={axis: peer}, device_id_type=MESH,
            ))
            copies[-1].start()
        return copies

    row_copies = spread(across, across_send, across_recv, in_row, "cls")

    spans = (pl.ds(0, rows // 2), pl.ds(rows // 2, rows // 2))

    def mine(j, h):
        return g_ref[2 * j + core, spans[h], :].astype(jnp.float32) + from_pair[j, spans[h], :].astype(jnp.float32)

    def ring(way, d, h):
        i = (way * far + d - 1) * 2 + h
        return pltpu.make_async_remote_copy(
            src_ref=going.at[way, d - 1, spans[h]], dst_ref=came.at[way, d - 1, spans[h]],
            send_sem=ring_send.at[i], recv_sem=ring_recv.at[i],
            device_id={"batch": at_distance(way, d if d < 3 else d - 2) * 2 + core}, device_id_type=MESH,
        )

    sent = []

    def send(way, d, h, value):
        going[way, d - 1, spans[h], :] = value.astype(jnp.bfloat16)
        sent.append(ring(way, d, h))
        sent[-1].start()

    def landed(way, d, h):
        ring(way, d, h).wait_recv()
        return came[way, d - 1, spans[h], :].astype(jnp.float32)

    pairs[far].wait_recv()
    for way in (0, 1):
        send(way, far, way, mine(at_distance(way, far), way))
    for d in (3, 1):
        if d == 1:
            for copy in row_copies:
                copy.wait_recv()
            down[0] = sum(across[d] for d in range(1, side)) + across[0]
            column_copies = spread(down, down_send, down_recv, in_column, "cls")
        for way in (0, 1):
            pairs[d if way == 0 else depth - d].wait_recv()
            for h in (0, 1):
                send(way, d, h, mine(at_distance(way, d), h))
        if d == 3:
            for way in (0, 1):
                pairs[2 if way == 0 else depth - 2].wait_recv()
    for h in (0, 1):
        for way in (0, 1):
            value = mine(at_distance(way, 2), h) + landed(way, 3, h)
            if h == way:
                value += landed(way, far, h)
            send(way, 2, h, value)

    lane = lax.broadcasted_iota(jnp.int32, (1, length), 1)
    count = jnp.sum(jnp.where(lane == me, counts_ref[0:1, :], 0.0), axis=1, keepdims=True)
    factor = STEP / (count + 1.0)
    pairs[0].wait_recv()
    for h in (0, 1):
        value = mine(z, h)
        for d in (1, 2):
            for way in (0, 1):
                value += landed(way, d, h)
        new_ref[0, spans[h], :] = vol_ref[0, spans[h], :].astype(jnp.float32) + value * factor
    for copy in column_copies:
        copy.wait_recv()
    scores_ref[...] = sum(down[d] for d in range(1, side)) + down[0]
    for copy in sent + row_copies + column_copies + list(pairs.values()):
        copy.wait_send()


def reduce_call(g, volumes, partial, counts, scale, lanes):
    devices, rows, length = g.shape
    depth = devices // 2
    far = depth // 2
    side = math.isqrt(lanes)
    inside = pl.BlockSpec(memory_space=pltpu.VMEM)
    sems = lambda n: pltpu.SemaphoreType.DMA((n,))
    peers = max(side - 1, 1)
    return pl.pallas_call(
        functools.partial(reduce_kernel, side, scale),
        out_shape=(
            jax.ShapeDtypeStruct((1, rows, length), jnp.float32),
            jax.ShapeDtypeStruct((8, partial.shape[0]), jnp.float32),
        ),
        in_specs=[inside] * 4,
        out_specs=(inside, inside),
        scratch_shapes=[
            pltpu.VMEM((depth, rows, length), jnp.bfloat16),
            pltpu.VMEM((2, far, rows, length), jnp.bfloat16),
            pltpu.VMEM((2, far, rows, length), jnp.bfloat16),
            pltpu.VMEM((side, 8, partial.shape[0]), jnp.float32),
            pltpu.VMEM((side, 8, partial.shape[0]), jnp.float32),
            sems(depth), sems(depth), sems(4 * far), sems(4 * far),
            sems(peers), sems(peers), sems(peers), sems(peers),
        ],
        compiler_params=pltpu.CompilerParams(collective_id=1, has_side_effects=True, vmem_limit_bytes=12 << 20),
        name="reduce",
    )(g, volumes, partial, counts)


def main_kernel(
    x_ref, a_ref, spec_ref, table_ref, class_in, orient_in, g_ref, sc_ref,
    v_ref, acc_ref, fwd_ref, high_ref, low_ref, cls_ref, ori_ref, sem,
):
    step = pl.program_id(0)
    block, rows, length = x_ref.shape
    classes = spec_ref.shape[0]
    period = a_ref.shape[1]
    unit = length // ORIENTS

    @pl.when(step == 0)
    def _():
        copies = [
            pltpu.make_async_copy(table_ref.at[:, pl.ds(0, 2 * length)], fwd_ref, sem.at[0]),
            pltpu.make_async_copy(table_ref.at[:, pl.ds(2 * length, length)], high_ref, sem.at[1]),
            pltpu.make_async_copy(table_ref.at[:, pl.ds(3 * length, length)], low_ref, sem.at[2]),
            pltpu.make_async_copy(class_in, cls_ref, sem.at[3]),
            pltpu.make_async_copy(orient_in, ori_ref, sem.at[4]),
        ]
        for copy in copies:
            copy.start()

        @pl.loop(0, classes)
        def _(k):
            v_ref[k] = spec_ref[k].astype(jnp.float32)
            acc_ref[k] = jnp.zeros(acc_ref.shape[1:], jnp.float32)

        for copy in copies:
            copy.wait()

    for i in range(block):
        p = step * block + i
        k = cls_ref[p]
        start = pl.multiple_of(length - unit * ori_ref[p], unit)
        y = jnp.dot(x_ref[i], fwd_ref[pl.ds(start, length), :], preferred_element_type=jnp.float32)
        totals = {}
        for r in range(0, period, 8):
            a = a_ref[i, r : r + 8, :]
            for j in range(r, rows, period):
                for c in (0, length):
                    d = y[j : j + 8, c : c + length] - a * v_ref[k, j : j + 8, c : c + length]
                    key = (j // period % 2, c)
                    totals[key] = totals[key] + d * d if key in totals else d * d
                    acc_ref[k, j : j + 8, c : c + length] += a * d
        total = sum(totals.values())
        sc_ref[i, :] = jnp.sum(total, axis=0)

    @pl.when(step == pl.num_programs(0) - 1)
    def _():
        @pl.loop(0, classes)
        def _(k):
            s = acc_ref[k]
            s_high = s.astype(jnp.bfloat16)
            s_low = (s - s_high.astype(jnp.float32)).astype(jnp.bfloat16)
            g = jnp.dot(s_high, high_ref[...], preferred_element_type=jnp.float32)
            g += jnp.dot(s_low, high_ref[...], preferred_element_type=jnp.float32)
            g += jnp.dot(s_high, low_ref[...], preferred_element_type=jnp.float32)
            g_ref[k] = g.astype(jnp.bfloat16)


def main_call(x, a, spectra, assignment, orientation, table):
    total, rows, length = x.shape
    classes = spectra.shape[0]
    period = a.shape[1]
    outside = pl.BlockSpec(memory_space=pltpu.HBM)
    return pl.pallas_call(
        main_kernel,
        out_shape=(
            jax.ShapeDtypeStruct((classes, rows, length), jnp.bfloat16),
            jax.ShapeDtypeStruct((total, length), jnp.float32),
        ),
        grid=(total // BLOCK,),
        in_specs=[
            pl.BlockSpec((BLOCK, rows, length), lambda i: (i, 0, 0)),
            pl.BlockSpec((BLOCK, period, length), lambda i: (i, 0, 0)),
            pl.BlockSpec((classes, rows, 2 * length), lambda i: (0, 0, 0)),
            outside, outside, outside,
        ],
        out_specs=[
            pl.BlockSpec((classes, rows, length), lambda i: (0, 0, 0)),
            pl.BlockSpec((BLOCK, length), lambda i: (i, 0)),
        ],
        scratch_shapes=[
            pltpu.VMEM((classes, rows, 2 * length), jnp.float32),
            pltpu.VMEM((classes, rows, 2 * length), jnp.float32),
            pltpu.VMEM((2 * length, 2 * length), jnp.bfloat16),
            pltpu.VMEM((2 * length, length), jnp.bfloat16),
            pltpu.VMEM((2 * length, length), jnp.bfloat16),
            pltpu.SMEM((total,), jnp.int32),
            pltpu.SMEM((total,), jnp.int32),
            pltpu.SemaphoreType.DMA((5,)),
        ],
        compiler_params=pltpu.CompilerParams(
            vmem_limit_bytes=44 << 20
        ),
        name="main",
    )(x, a, spectra, table, assignment, orientation)


def local(particles, volumes, assignment, defocus, tilt_limits, orientation):
    total, rows, length = particles.shape
    devices = lax.axis_size("batch")
    lanes = lax.axis_size("cls")
    assert volumes.shape[0] == 1 and rows % (length // 2) == 0
    table = tables(length)
    hbm = lambda v: pltpu.with_memory_space_constraint(v, pltpu.HBM)
    volumes, assignment, defocus, tilt_limits, table, orientation, particles = map(
        hbm, (volumes, assignment, defocus, tilt_limits, table, orientation, particles)
    )
    spectra, a, tally = gather_call(volumes, assignment, defocus, tilt_limits, table, devices)
    g, partial = main_call(particles, a, spectra, assignment, orientation, table)
    scale = 1.0 / (rows * lanes * length * length)
    updated, scores = reduce_call(g, volumes, partial, tally, scale, lanes)
    return updated, scores[0]


def solution(mesh):
    in_specs = (
        P("batch", "cls", None),
        P("batch", "cls", None),
        P("batch"),
        P("batch"),
        P("batch", None),
        P("batch"),
    )
    out_specs = (P("batch", "cls", None), P("batch"))
    return jax.shard_map(local, mesh=mesh, in_specs=in_specs, out_specs=out_specs, check_vma=False)
```

```python
import functools
import math

import jax
import jax.numpy as jnp
import numpy as np
from jax import lax
from jax.experimental import pallas as pl
from jax.experimental.pallas import tpu as pltpu
from jax.sharding import PartitionSpec as P

ORIENTS = 8
STEP = 0.5
PHASE = 0.1
BLOCK = 16


def tables(length):
    index = np.arange(length)
    angle = 2.0 * np.pi * ((index[:, None] * index[None, :]) % length) / length
    cosine, sine = np.cos(angle), np.sin(angle)
    forward = np.concatenate([cosine, -sine], axis=1).astype(np.float32)
    back = (np.concatenate([cosine, -sine], axis=0) / length).astype(np.float32)
    turned = jnp.asarray(np.concatenate([forward, forward], axis=0)).astype(jnp.bfloat16)
    back = jnp.asarray(back)
    high = back.astype(jnp.bfloat16)
    low = (back - high.astype(jnp.float32)).astype(jnp.bfloat16)
    return jnp.concatenate([turned, high, low], axis=1)


MESH = pl.DeviceIdType.MESH


def sine_terms(count):
    u = np.cos(np.pi * (np.arange(4000) + 0.5) / 4000) * 0.5
    u = u[np.abs(u) > 1e-6]
    basis = np.stack([u ** (2 * i + 1) for i in range(count)], axis=1)
    return [float(c) for c in np.linalg.lstsq(basis, -np.sin(2 * np.pi * u), rcond=None)[0]]


def gather_kernel(
    defocus_in, tilt_in, class_in, vol_ref, table_ref, v_out, a_out, counts_out,
    buf, v_buf, a_buf, tally_buf, fwd_ref, tilt_ref, defocus_ref, class_ref,
    own_sem, v_sem, a_sem, ring_send, ring_recv, pair_send, pair_recv,
):
    devices, _, length = buf.shape
    rows = vol_ref.shape[1]
    total, period, _ = a_buf.shape
    depth = devices // 2
    far = depth // 2
    me = lax.axis_index("batch")
    z, core = me // 2, me % 2
    other = 1 - core
    partner = z * 2 + other

    def at_distance(way, d):
        return (z + d) % depth if way == 0 else (z + depth - d) % depth

    own = [
        pltpu.make_async_copy(class_in, class_ref, own_sem.at[0]),
        pltpu.make_async_copy(vol_ref.at[0], buf.at[me, pl.ds(0, rows)], own_sem.at[1]),
        pltpu.make_async_copy(defocus_in, defocus_ref, own_sem.at[2]),
        pltpu.make_async_copy(tilt_in, tilt_ref, own_sem.at[3]),
        pltpu.make_async_copy(table_ref.at[pl.ds(0, length), pl.ds(0, 2 * length)], fwd_ref, own_sem.at[4]),
    ]
    for copy in own:
        copy.start()
    barrier = pltpu.get_barrier_semaphore()
    for way, d in ((0, 1), (1, 1), (0, 2), (1, 2)):
        peer = at_distance(way, d) * 2 + core
        pl.semaphore_signal(barrier, inc=1, device_id={"batch": peer}, device_id_type=MESH)
    pl.semaphore_signal(barrier, inc=1, device_id={"batch": partner}, device_id_type=MESH)
    ids = lax.broadcasted_iota(jnp.int32, tally_buf.shape, 1)

    def count(p, tally):
        return tally + jnp.where(ids == class_ref[p], 1.0, 0.0)

    own[0].wait()
    tally = lax.fori_loop(0, total, count, jnp.zeros(ids.shape, jnp.float32), unroll=8)
    tally_buf[...] = tally.astype(jnp.bfloat16)
    own.append(pltpu.make_async_copy(tally_buf, buf.at[me, pl.ds(rows, tally_buf.shape[0])], own_sem.at[5]))
    own[-1].start()
    for copy in own[1:]:
        copy.wait()
    freq = lax.broadcasted_iota(jnp.int32, (8, length), 1)
    row = lax.broadcasted_iota(jnp.int32, (8, length), 0)
    signed = jnp.where(freq < length // 2, freq, freq - length)
    reach = (8 * jnp.abs(signed)).astype(jnp.float32)
    half = length // 2
    along_s = (signed * signed).astype(jnp.float32) * (0.5 / (half * half))
    lane_radius = 8 * (freq % 8) + row + 1
    along_r = (lane_radius * lane_radius).astype(jnp.float32) * (0.5 / (half * half))
    radii = [(row + (1 + r)).astype(jnp.float32) for r in range(0, period, 8)]
    phase = PHASE / (2.0 * math.pi)
    terms = sine_terms(7)

    def minus_sine(turns):
        u = turns - jnp.floor(turns + 0.5)
        w = u * u
        s = jnp.full_like(w, terms[-1])
        for c in terms[-2::-1]:
            s = s * w + c
        return s * u

    group = length // 8
    groups = total // group
    bounds = [q * groups // (far + 1) for q in range(far + 2)]
    a_copies = []

    def filters(q):
        first, last = bounds[q], bounds[q + 1]

        def body(b, carry):
            base = b * group
            ds = [defocus_ref[base + i] for i in range(group)]
            by_lane = jnp.full((8, length), ds[0], jnp.float32)
            for i in range(1, group):
                by_lane = jnp.where(freq >= 8 * i, ds[i], by_lane)
            turns_r = by_lane * along_r
            sine_r = minus_sine(turns_r)
            cosine_r = minus_sine(turns_r + 0.25)
            for e in range(0, group, 8):
                by_row = jnp.full((8, length), ds[e], jnp.float32)
                for i in range(1, 8):
                    by_row = jnp.where(row >= i, ds[e + i], by_row)
                turns_s = by_row * along_s + phase
                sine_s = minus_sine(turns_s)
                cosine_s = minus_sine(turns_s + 0.25)
                for i in range(8):
                    at = 8 * (e + i)
                    ss = jnp.broadcast_to(sine_s[i : i + 1, :], (8, length))
                    cs = jnp.broadcast_to(cosine_s[i : i + 1, :], (8, length))
                    p = base + e + i
                    limit = jnp.where(freq < length // 2, tilt_ref[p], tilt_ref[total + p]).astype(jnp.float32)
                    for n in range(period // 8):
                        sr = jnp.broadcast_to(sine_r[:, at + n : at + n + 1], (8, length))
                        cr = jnp.broadcast_to(cosine_r[:, at + n : at + n + 1], (8, length))
                        keep = reach <= limit * radii[n]
                        a_buf[base + e + i, 8 * n : 8 * n + 8, :] = jnp.where(keep, -(ss * cr + cs * sr), 0.0)
            return carry

        lax.fori_loop(first, last, body, 0)
        at = pl.ds(first * group, (last - first) * group)
        if last > first:
            a_copies.append(pltpu.make_async_copy(a_buf.at[at], a_out.at[at], a_sem.at[q]))
            a_copies[-1].start()

    filters(0)
    filters(1)
    pl.semaphore_wait(barrier, 5)

    spans = (pl.ds(0, rows // 2), pl.ds(rows // 2, buf.shape[1] - rows // 2))

    def halves(way, d):
        return (0, 1) if d < far else (way,)

    def unit(way, d, h):
        return (way * far + d - 1) * 2 + h

    def ring(way, d, h, first):
        at = buf.at[at_distance(1 - way, first) * 2 + core, spans[h]]
        i = unit(way, d, h)
        return pltpu.make_async_remote_copy(
            src_ref=at, dst_ref=at, send_sem=ring_send.at[i], recv_sem=ring_recv.at[i],
            device_id={"batch": at_distance(way, d - first) * 2 + core}, device_id_type=MESH,
        )

    def arrival(way, d, h):
        at = buf.at[at_distance(1 - way, d) * 2 + core, spans[h]]
        i = unit(way, d, h)
        return pltpu.make_async_remote_copy(
            src_ref=at, dst_ref=at, send_sem=ring_send.at[i], recv_sem=ring_recv.at[i],
            device_id={"batch": at_distance(way, 1) * 2 + core}, device_id_type=MESH,
        )

    def pair(zz, i, h, which):
        at = buf.at[zz * 2 + which, spans[h]]
        return pltpu.make_async_remote_copy(
            src_ref=at, dst_ref=at, send_sem=pair_send.at[i], recv_sem=pair_recv.at[i],
            device_id={"batch": partner}, device_id_type=MESH,
        )

    sent = []
    own_unit = 4 * far

    def send(copy):
        copy.start()
        sent.append(copy)

    for d in (2, 1):
        for h in (0, 1):
            for way in (0, 1):
                send(ring(way, d, h, 0))
    for h in (0, 1):
        send(pair(z, own_unit + h, h, core))

    v_copies = []

    def transform(slot, i):
        spectrum = jnp.dot(buf[slot, 0:rows, :], fwd_ref[0:length, :], preferred_element_type=jnp.float32)
        v_buf[slot] = spectrum.astype(jnp.bfloat16)
        copy = pltpu.make_async_copy(v_buf.at[slot], v_out.at[slot], v_sem.at[i])
        copy.start()
        v_copies.append(copy)

    def arrived(d):
        for h in (0, 1):
            for way in (0, 1):
                if h not in halves(way, d):
                    continue
                arrival(way, d, h).wait_recv()
                if d == 2:
                    send(ring(way, 3, h, 2))
                    if h in halves(way, far):
                        send(ring(way, far, h, 2))
        for h in (0, 1):
            for way in (0, 1):
                if h in halves(way, d):
                    send(pair(at_distance(1 - way, d), unit(way, d, h), h, core))

    def ours(d):
        for way in (0, 1) if d < far else (0,):
            transform(at_distance(1 - way, d) * 2 + core, len(v_copies))

    def theirs(d):
        if d == 0:
            for h in (0, 1):
                pair(z, own_unit + h, h, other).wait_recv()
            transform(partner, len(v_copies))
            return
        for way in (0, 1):
            for h in halves(way, d):
                pair(at_distance(1 - way, d), unit(way, d, h), h, other).wait_recv()
        for way in (0, 1) if d < far else (0,):
            transform(at_distance(1 - way, d) * 2 + other, len(v_copies))

    transform(me, 0)
    filters(2)
    arrived(2)
    filters(3)
    arrived(1)
    filters(4)
    theirs(0)
    ours(2)
    ours(1)
    arrived(3)
    theirs(2)
    arrived(far)
    theirs(1)
    ours(3)
    ours(far)
    theirs(3)
    theirs(far)
    tally = jnp.zeros((8, length), jnp.float32)
    for b in range(devices):
        tally += buf[b, rows : rows + 8, :].astype(jnp.float32)
    counts_out[...] = tally
    for copy in sent:
        copy.wait_send()
    for copy in v_copies + a_copies:
        copy.wait()


def gather_call(volumes, assignment, defocus, tilts, table, devices):
    _, rows, length = volumes.shape
    total = defocus.shape[0]
    period = length // 2
    assert devices == 16
    anywhere = pl.BlockSpec(memory_space=pl.ANY)
    inside = pl.BlockSpec(memory_space=pltpu.VMEM)
    sems = lambda n: pltpu.SemaphoreType.DMA((n,))
    return pl.pallas_call(
        gather_kernel,
        out_shape=(
            jax.ShapeDtypeStruct((devices, rows, 2 * length), jnp.bfloat16),
            jax.ShapeDtypeStruct((total, period, length), jnp.float32),
            jax.ShapeDtypeStruct((8, length), jnp.float32),
        ),
        in_specs=[pl.BlockSpec(memory_space=pltpu.HBM)] * 5,
        out_specs=(anywhere, anywhere, inside),
        scratch_shapes=[
            pltpu.VMEM((devices, rows + 16, length), jnp.bfloat16),
            pltpu.VMEM((devices, rows, 2 * length), jnp.bfloat16),
            pltpu.VMEM((total, period, length), jnp.float32),
            pltpu.VMEM((16, length), jnp.bfloat16),
            pltpu.VMEM((length, 2 * length), jnp.bfloat16),
            pltpu.SMEM((2 * total,), jnp.int32),
            pltpu.SMEM((total,), jnp.float32),
            pltpu.SMEM((total,), jnp.int32),
            sems(6), sems(devices), sems(5),
            sems(devices), sems(devices), sems(devices + 2), sems(devices + 2),
        ],
        compiler_params=pltpu.CompilerParams(collective_id=0, has_side_effects=True, vmem_limit_bytes=16 << 20),
        name="gather",
    )(defocus, tilts, assignment, volumes, table)


def reduce_kernel(
    side, scale, g_ref, vol_ref, sc_ref, counts_ref, new_ref, scores_ref,
    from_pair, came, going, across, down,
    pair_send, pair_recv, ring_send, ring_recv, across_send, across_recv, down_send, down_recv,
):
    devices, rows, length = g_ref.shape
    depth = devices // 2
    far = depth // 2
    me = lax.axis_index("batch")
    z, core = me // 2, me % 2
    other = 1 - core
    partner = z * 2 + other
    c = lax.axis_index("cls")
    y, x = c // side, c % side
    in_row = [y * side + (x + d) % side for d in range(1, side)]
    in_column = [((y + d) % side) * side + x for d in range(1, side)]

    def at_distance(way, d):
        return (z + d) % depth if way == 0 else (z + depth - d) % depth

    barrier = pltpu.get_barrier_semaphore()
    for way, d in ((0, 1), (1, 1), (0, 2), (1, 2)):
        peer = at_distance(way, d) * 2 + core
        pl.semaphore_signal(barrier, inc=1, device_id={"batch": peer}, device_id_type=MESH)
    pl.semaphore_signal(barrier, inc=1, device_id={"batch": partner}, device_id_type=MESH)
    for peer in in_row + in_column:
        pl.semaphore_signal(barrier, inc=1, device_id={"cls": peer}, device_id_type=MESH)
    across[0] = lax.dot_general(
        jnp.full((8, length), scale, jnp.float32), sc_ref[...], (((1,), (1,)), ((), ())),
        precision=lax.Precision.HIGHEST, preferred_element_type=jnp.float32,
    )
    pl.semaphore_wait(barrier, 5 + 2 * (side - 1))

    order = [far]
    for d in range(far - 1, 0, -1):
        order += [d, depth - d]
    order.append(0)
    pairs = {}
    for i, d in enumerate(order):
        j = (z + d) % depth
        pairs[d] = pltpu.make_async_remote_copy(
            src_ref=g_ref.at[2 * j + other], dst_ref=from_pair.at[j],
            send_sem=pair_send.at[i], recv_sem=pair_recv.at[i],
            device_id={"batch": partner}, device_id_type=MESH,
        )
        pairs[d].start()

    def spread(ref, send, recv, peers, axis):
        copies = []
        for d, peer in enumerate(peers, 1):
            copies.append(pltpu.make_async_remote_copy(
                src_ref=ref.at[0], dst_ref=ref.at[d], send_sem=send.at[d - 1], recv_sem=recv.at[d - 1],
                device_id={axis: peer}, device_id_type=MESH,
            ))
            copies[-1].start()
        return copies

    row_copies = spread(across, across_send, across_recv, in_row, "cls")

    spans = (pl.ds(0, rows // 2), pl.ds(rows // 2, rows // 2))

    def mine(j, h):
        return g_ref[2 * j + core, spans[h], :].astype(jnp.float32) + from_pair[j, spans[h], :].astype(jnp.float32)

    def ring(way, d, h):
        i = (way * far + d - 1) * 2 + h
        return pltpu.make_async_remote_copy(
            src_ref=going.at[way, d - 1, spans[h]], dst_ref=came.at[way, d - 1, spans[h]],
            send_sem=ring_send.at[i], recv_sem=ring_recv.at[i],
            device_id={"batch": at_distance(way, d if d < 3 else d - 2) * 2 + core}, device_id_type=MESH,
        )

    sent = []

    def send(way, d, h, value):
        going[way, d - 1, spans[h], :] = value.astype(jnp.bfloat16)
        sent.append(ring(way, d, h))
        sent[-1].start()

    def landed(way, d, h):
        ring(way, d, h).wait_recv()
        return came[way, d - 1, spans[h], :].astype(jnp.float32)

    pairs[far].wait_recv()
    for way in (0, 1):
        send(way, far, way, mine(at_distance(way, far), way))
    for d in (3, 1):
        if d == 1:
            for copy in row_copies:
                copy.wait_recv()
            down[0] = sum(across[d] for d in range(1, side)) + across[0]
            column_copies = spread(down, down_send, down_recv, in_column, "cls")
        for way in (0, 1):
            pairs[d if way == 0 else depth - d].wait_recv()
            for h in (0, 1):
                send(way, d, h, mine(at_distance(way, d), h))
        if d == 3:
            for way in (0, 1):
                pairs[2 if way == 0 else depth - 2].wait_recv()
    for h in (0, 1):
        for way in (0, 1):
            value = mine(at_distance(way, 2), h) + landed(way, 3, h)
            if h == way:
                value += landed(way, far, h)
            send(way, 2, h, value)

    lane = lax.broadcasted_iota(jnp.int32, (1, length), 1)
    count = jnp.sum(jnp.where(lane == me, counts_ref[0:1, :], 0.0), axis=1, keepdims=True)
    factor = STEP / (count + 1.0)
    pairs[0].wait_recv()
    for h in (0, 1):
        value = mine(z, h)
        for d in (1, 2):
            for way in (0, 1):
                value += landed(way, d, h)
        new_ref[0, spans[h], :] = vol_ref[0, spans[h], :].astype(jnp.float32) + value * factor
    for copy in column_copies:
        copy.wait_recv()
    scores_ref[...] = sum(down[d] for d in range(1, side)) + down[0]
    for copy in sent + row_copies + column_copies + list(pairs.values()):
        copy.wait_send()


def reduce_call(g, volumes, partial, counts, scale, lanes):
    devices, rows, length = g.shape
    depth = devices // 2
    far = depth // 2
    side = math.isqrt(lanes)
    inside = pl.BlockSpec(memory_space=pltpu.VMEM)
    sems = lambda n: pltpu.SemaphoreType.DMA((n,))
    peers = max(side - 1, 1)
    return pl.pallas_call(
        functools.partial(reduce_kernel, side, scale),
        out_shape=(
            jax.ShapeDtypeStruct((1, rows, length), jnp.float32),
            jax.ShapeDtypeStruct((8, partial.shape[0]), jnp.float32),
        ),
        in_specs=[inside] * 4,
        out_specs=(inside, inside),
        scratch_shapes=[
            pltpu.VMEM((depth, rows, length), jnp.bfloat16),
            pltpu.VMEM((2, far, rows, length), jnp.bfloat16),
            pltpu.VMEM((2, far, rows, length), jnp.bfloat16),
            pltpu.VMEM((side, 8, partial.shape[0]), jnp.float32),
            pltpu.VMEM((side, 8, partial.shape[0]), jnp.float32),
            sems(depth), sems(depth), sems(4 * far), sems(4 * far),
            sems(peers), sems(peers), sems(peers), sems(peers),
        ],
        compiler_params=pltpu.CompilerParams(collective_id=1, has_side_effects=True, vmem_limit_bytes=12 << 20),
        name="reduce",
    )(g, volumes, partial, counts)


def main_kernel(
    x_ref, a_ref, spec_ref, table_ref, class_in, orient_in, g_ref, sc_ref,
    v_ref, acc_ref, fwd_ref, high_ref, low_ref, cls_ref, ori_ref, sem,
):
    step = pl.program_id(0)
    block, rows, length = x_ref.shape
    classes = spec_ref.shape[0]
    period = a_ref.shape[1]
    unit = length // ORIENTS

    @pl.when(step == 0)
    def _():
        copies = [
            pltpu.make_async_copy(table_ref.at[:, pl.ds(0, 2 * length)], fwd_ref, sem.at[0]),
            pltpu.make_async_copy(table_ref.at[:, pl.ds(2 * length, length)], high_ref, sem.at[1]),
            pltpu.make_async_copy(table_ref.at[:, pl.ds(3 * length, length)], low_ref, sem.at[2]),
            pltpu.make_async_copy(class_in, cls_ref, sem.at[3]),
            pltpu.make_async_copy(orient_in, ori_ref, sem.at[4]),
        ]
        for copy in copies:
            copy.start()

        @pl.loop(0, classes)
        def _(k):
            v_ref[k] = spec_ref[k].astype(jnp.float32)
            acc_ref[k] = jnp.zeros(acc_ref.shape[1:], jnp.float32)

        for copy in copies:
            copy.wait()

    for i in range(block):
        p = step * block + i
        k = cls_ref[p]
        start = pl.multiple_of(length - unit * ori_ref[p], unit)
        y = jnp.dot(x_ref[i], fwd_ref[pl.ds(start, length), :], preferred_element_type=jnp.float32)
        totals = {}
        for r in range(0, period, 8):
            a = a_ref[i, r : r + 8, :]
            for j in range(r, rows, period):
                for c in (0, length):
                    d = y[j : j + 8, c : c + length] - a * v_ref[k, j : j + 8, c : c + length]
                    key = (j // period % 2, c)
                    totals[key] = totals[key] + d * d if key in totals else d * d
                    acc_ref[k, j : j + 8, c : c + length] += a * d
        total = sum(totals.values())
        sc_ref[i, :] = jnp.sum(total, axis=0)

    @pl.when(step == pl.num_programs(0) - 1)
    def _():
        @pl.loop(0, classes)
        def _(k):
            s = acc_ref[k]
            s_high = s.astype(jnp.bfloat16)
            s_low = (s - s_high.astype(jnp.float32)).astype(jnp.bfloat16)
            g = jnp.dot(s_high, high_ref[...], preferred_element_type=jnp.float32)
            g += jnp.dot(s_low, high_ref[...], preferred_element_type=jnp.float32)
            g += jnp.dot(s_high, low_ref[...], preferred_element_type=jnp.float32)
            g_ref[k] = g.astype(jnp.bfloat16)


def main_call(x, a, spectra, assignment, orientation, table):
    total, rows, length = x.shape
    classes = spectra.shape[0]
    period = a.shape[1]
    outside = pl.BlockSpec(memory_space=pltpu.HBM)
    return pl.pallas_call(
        main_kernel,
        out_shape=(
            jax.ShapeDtypeStruct((classes, rows, length), jnp.bfloat16),
            jax.ShapeDtypeStruct((total, length), jnp.float32),
        ),
        grid=(total // BLOCK,),
        in_specs=[
            pl.BlockSpec((BLOCK, rows, length), lambda i: (i, 0, 0)),
            pl.BlockSpec((BLOCK, period, length), lambda i: (i, 0, 0)),
            pl.BlockSpec((classes, rows, 2 * length), lambda i: (0, 0, 0)),
            outside, outside, outside,
        ],
        out_specs=[
            pl.BlockSpec((classes, rows, length), lambda i: (0, 0, 0)),
            pl.BlockSpec((BLOCK, length), lambda i: (i, 0)),
        ],
        scratch_shapes=[
            pltpu.VMEM((classes, rows, 2 * length), jnp.float32),
            pltpu.VMEM((classes, rows, 2 * length), jnp.float32),
            pltpu.VMEM((2 * length, 2 * length), jnp.bfloat16),
            pltpu.VMEM((2 * length, length), jnp.bfloat16),
            pltpu.VMEM((2 * length, length), jnp.bfloat16),
            pltpu.SMEM((total,), jnp.int32),
            pltpu.SMEM((total,), jnp.int32),
            pltpu.SemaphoreType.DMA((5,)),
        ],
        compiler_params=pltpu.CompilerParams(
            vmem_limit_bytes=44 << 20
        ),
        name="main",
    )(x, a, spectra, table, assignment, orientation)


def local(particles, volumes, assignment, defocus, tilt_limits, orientation):
    total, rows, length = particles.shape
    devices = lax.axis_size("batch")
    lanes = lax.axis_size("cls")
    assert volumes.shape[0] == 1 and rows % (length // 2) == 0
    table = tables(length)
    tilt_limits = tilt_limits.T.reshape(2 * total)
    hbm = lambda v: pltpu.with_memory_space_constraint(v, pltpu.HBM)
    volumes, assignment, defocus, tilt_limits, table, orientation, particles = map(
        hbm, (volumes, assignment, defocus, tilt_limits, table, orientation, particles)
    )
    spectra, a, tally = gather_call(volumes, assignment, defocus, tilt_limits, table, devices)
    g, partial = main_call(particles, a, spectra, assignment, orientation, table)
    scale = 1.0 / (rows * lanes * length * length)
    updated, scores = reduce_call(g, volumes, partial, tally, scale, lanes)
    return updated, scores[0]


def solution(mesh):
    in_specs = (
        P("batch", "cls", None),
        P("batch", "cls", None),
        P("batch"),
        P("batch"),
        P("batch", None),
        P("batch"),
    )
    out_specs = (P("batch", "cls", None), P("batch"))
    return jax.shard_map(local, mesh=mesh, in_specs=in_specs, out_specs=out_specs, check_vma=False)
```

```python
import functools
import math

import jax
import jax.numpy as jnp
import numpy as np
from jax import lax
from jax.experimental import pallas as pl
from jax.experimental.pallas import tpu as pltpu
from jax.sharding import PartitionSpec as P

ORIENTS = 8
STEP = 0.5
PHASE = 0.1
BLOCK = 16


def tables(length):
    index = np.arange(length)
    angle = 2.0 * np.pi * ((index[:, None] * index[None, :]) % length) / length
    cosine, sine = np.cos(angle), np.sin(angle)
    forward = np.concatenate([cosine, -sine], axis=1).astype(np.float32)
    back = (np.concatenate([cosine, -sine], axis=0) / length).astype(np.float32)
    turned = jnp.asarray(np.concatenate([forward, forward], axis=0)).astype(jnp.bfloat16)
    back = jnp.asarray(back)
    high = back.astype(jnp.bfloat16)
    low = (back - high.astype(jnp.float32)).astype(jnp.bfloat16)
    return jnp.concatenate([turned, high, low], axis=1)


MESH = pl.DeviceIdType.MESH


def sine_terms(count):
    u = np.cos(np.pi * (np.arange(4000) + 0.5) / 4000) * 0.5
    u = u[np.abs(u) > 1e-6]
    basis = np.stack([u ** (2 * i + 1) for i in range(count)], axis=1)
    return [float(c) for c in np.linalg.lstsq(basis, -np.sin(2 * np.pi * u), rcond=None)[0]]


def gather_kernel(
    defocus_in, tilt_in, class_in, vol_ref, table_ref, v_out, a_out, counts_out,
    buf, v_buf, a_buf, tally_buf, fwd_ref, tilt_ref, defocus_ref, class_ref,
    own_sem, v_sem, a_sem, ring_send, ring_recv, pair_send, pair_recv,
):
    devices, _, length = buf.shape
    rows = vol_ref.shape[1]
    total, period, _ = a_buf.shape
    depth = devices // 2
    far = depth // 2
    me = lax.axis_index("batch")
    z, core = me // 2, me % 2
    other = 1 - core
    partner = z * 2 + other

    def at_distance(way, d):
        return (z + d) % depth if way == 0 else (z + depth - d) % depth

    own = [
        pltpu.make_async_copy(class_in, class_ref, own_sem.at[0]),
        pltpu.make_async_copy(vol_ref.at[0], buf.at[me, pl.ds(0, rows)], own_sem.at[1]),
        pltpu.make_async_copy(defocus_in, defocus_ref, own_sem.at[2]),
        pltpu.make_async_copy(tilt_in, tilt_ref, own_sem.at[3]),
        pltpu.make_async_copy(table_ref.at[pl.ds(0, length), pl.ds(0, 2 * length)], fwd_ref, own_sem.at[4]),
    ]
    for copy in own:
        copy.start()
    barrier = pltpu.get_barrier_semaphore()
    for way, d in ((0, 1), (1, 1), (0, 2), (1, 2)):
        peer = at_distance(way, d) * 2 + core
        pl.semaphore_signal(barrier, inc=1, device_id={"batch": peer}, device_id_type=MESH)
    pl.semaphore_signal(barrier, inc=1, device_id={"batch": partner}, device_id_type=MESH)
    ids = lax.broadcasted_iota(jnp.int32, tally_buf.shape, 1)

    def count(p, tally):
        return tally + jnp.where(ids == class_ref[p], 1.0, 0.0)

    own[0].wait()
    tally = lax.fori_loop(0, total, count, jnp.zeros(ids.shape, jnp.float32), unroll=8)
    tally_buf[...] = tally.astype(jnp.bfloat16)
    own.append(pltpu.make_async_copy(tally_buf, buf.at[me, pl.ds(rows, tally_buf.shape[0])], own_sem.at[5]))
    own[-1].start()
    for copy in own[1:]:
        copy.wait()
    freq = lax.broadcasted_iota(jnp.int32, (8, length), 1)
    row = lax.broadcasted_iota(jnp.int32, (8, length), 0)
    signed = jnp.where(freq < length // 2, freq, freq - length)
    reach = (8 * jnp.abs(signed)).astype(jnp.float32)
    half = length // 2
    along_s = (signed * signed).astype(jnp.float32) * (0.5 / (half * half))
    lane_radius = 8 * (freq % 8) + row + 1
    along_r = (lane_radius * lane_radius).astype(jnp.float32) * (0.5 / (half * half))
    radii = [(row + (1 + r)).astype(jnp.float32) for r in range(0, period, 8)]
    phase = PHASE / (2.0 * math.pi)
    terms = sine_terms(7)

    def minus_sine(turns):
        u = turns - jnp.floor(turns + 0.5)
        w = u * u
        s = jnp.full_like(w, terms[-1])
        for c in terms[-2::-1]:
            s = s * w + c
        return s * u

    group = length // 8
    groups = total // group
    bounds = [q * groups // (far + 1) for q in range(far + 2)]
    a_copies = []

    def filters(q):
        first, last = bounds[q], bounds[q + 1]

        def body(b, carry):
            base = b * group
            ds = [defocus_ref[base + i] for i in range(group)]
            by_lane = jnp.full((8, length), ds[0], jnp.float32)
            for i in range(1, group):
                by_lane = jnp.where(freq >= 8 * i, ds[i], by_lane)
            turns_r = by_lane * along_r
            sine_r = minus_sine(turns_r)
            cosine_r = minus_sine(turns_r + 0.25)
            for e in range(0, group, 8):
                by_row = jnp.full((8, length), ds[e], jnp.float32)
                for i in range(1, 8):
                    by_row = jnp.where(row >= i, ds[e + i], by_row)
                turns_s = by_row * along_s + phase
                sine_s = minus_sine(turns_s)
                cosine_s = minus_sine(turns_s + 0.25)
                for i in range(8):
                    at = 8 * (e + i)
                    ss = jnp.broadcast_to(sine_s[i : i + 1, :], (8, length))
                    cs = jnp.broadcast_to(cosine_s[i : i + 1, :], (8, length))
                    p = base + e + i
                    limit = jnp.where(freq < length // 2, tilt_ref[p], tilt_ref[total + p]).astype(jnp.float32)
                    for n in range(period // 8):
                        sr = jnp.broadcast_to(sine_r[:, at + n : at + n + 1], (8, length))
                        cr = jnp.broadcast_to(cosine_r[:, at + n : at + n + 1], (8, length))
                        keep = reach <= limit * radii[n]
                        a_buf[base + e + i, 8 * n : 8 * n + 8, :] = jnp.where(keep, -(ss * cr + cs * sr), 0.0)
            return carry

        lax.fori_loop(first, last, body, 0)
        at = pl.ds(first * group, (last - first) * group)
        if last > first:
            a_copies.append(pltpu.make_async_copy(a_buf.at[at], a_out.at[at], a_sem.at[q]))
            a_copies[-1].start()

    filters(0)
    filters(1)
    pl.semaphore_wait(barrier, 5)

    spans = (pl.ds(0, rows // 2), pl.ds(rows // 2, buf.shape[1] - rows // 2))

    def halves(way, d):
        return (0, 1) if d < far else (way,)

    def unit(way, d, h):
        return (way * far + d - 1) * 2 + h

    def ring(way, d, h, first):
        at = buf.at[at_distance(1 - way, first) * 2 + core, spans[h]]
        i = unit(way, d, h)
        return pltpu.make_async_remote_copy(
            src_ref=at, dst_ref=at, send_sem=ring_send.at[i], recv_sem=ring_recv.at[i],
            device_id={"batch": at_distance(way, d - first) * 2 + core}, device_id_type=MESH,
        )

    def arrival(way, d, h):
        at = buf.at[at_distance(1 - way, d) * 2 + core, spans[h]]
        i = unit(way, d, h)
        return pltpu.make_async_remote_copy(
            src_ref=at, dst_ref=at, send_sem=ring_send.at[i], recv_sem=ring_recv.at[i],
            device_id={"batch": at_distance(way, 1) * 2 + core}, device_id_type=MESH,
        )

    def pair(zz, i, h, which):
        at = buf.at[zz * 2 + which, spans[h]]
        return pltpu.make_async_remote_copy(
            src_ref=at, dst_ref=at, send_sem=pair_send.at[i], recv_sem=pair_recv.at[i],
            device_id={"batch": partner}, device_id_type=MESH,
        )

    sent = []
    own_unit = 4 * far

    def send(copy):
        copy.start()
        sent.append(copy)

    for d in (2, 1):
        for h in (0, 1):
            for way in (0, 1):
                send(ring(way, d, h, 0))
    for h in (0, 1):
        send(pair(z, own_unit + h, h, core))

    v_copies = []

    def transform(slot, i):
        spectrum = jnp.dot(buf[slot, 0:rows, :], fwd_ref[0:length, :], preferred_element_type=jnp.float32)
        v_buf[slot] = spectrum.astype(jnp.bfloat16)
        copy = pltpu.make_async_copy(v_buf.at[slot], v_out.at[slot], v_sem.at[i])
        copy.start()
        v_copies.append(copy)

    def arrived(d):
        for h in (0, 1):
            for way in (0, 1):
                if h not in halves(way, d):
                    continue
                arrival(way, d, h).wait_recv()
                if d == 2:
                    send(ring(way, 3, h, 2))
                    if h in halves(way, far):
                        send(ring(way, far, h, 2))
        for h in (0, 1):
            for way in (0, 1):
                if h in halves(way, d):
                    send(pair(at_distance(1 - way, d), unit(way, d, h), h, core))

    def ours(d):
        for way in (0, 1) if d < far else (0,):
            transform(at_distance(1 - way, d) * 2 + core, len(v_copies))

    def theirs(d):
        if d == 0:
            for h in (0, 1):
                pair(z, own_unit + h, h, other).wait_recv()
            transform(partner, len(v_copies))
            return
        for way in (0, 1):
            for h in halves(way, d):
                pair(at_distance(1 - way, d), unit(way, d, h), h, other).wait_recv()
        for way in (0, 1) if d < far else (0,):
            transform(at_distance(1 - way, d) * 2 + other, len(v_copies))

    transform(me, 0)
    filters(2)
    arrived(2)
    filters(3)
    arrived(1)
    filters(4)
    theirs(0)
    ours(2)
    ours(1)
    arrived(3)
    theirs(2)
    arrived(far)
    theirs(1)
    ours(3)
    ours(far)
    theirs(3)
    theirs(far)
    tally = jnp.zeros((8, length), jnp.float32)
    for b in range(devices):
        tally += buf[b, rows : rows + 8, :].astype(jnp.float32)
    counts_out[...] = tally
    for copy in sent:
        copy.wait_send()
    for copy in v_copies + a_copies:
        copy.wait()


def gather_call(volumes, assignment, defocus, tilts, table, devices):
    _, rows, length = volumes.shape
    total = defocus.shape[0]
    period = length // 2
    assert devices == 16
    anywhere = pl.BlockSpec(memory_space=pl.ANY)
    inside = pl.BlockSpec(memory_space=pltpu.VMEM)
    sems = lambda n: pltpu.SemaphoreType.DMA((n,))
    return pl.pallas_call(
        gather_kernel,
        out_shape=(
            jax.ShapeDtypeStruct((devices, rows, 2 * length), jnp.bfloat16),
            jax.ShapeDtypeStruct((total, period, length), jnp.float32),
            jax.ShapeDtypeStruct((8, length), jnp.float32),
        ),
        in_specs=[pl.BlockSpec(memory_space=pltpu.HBM)] * 5,
        out_specs=(anywhere, anywhere, inside),
        scratch_shapes=[
            pltpu.VMEM((devices, rows + 16, length), jnp.bfloat16),
            pltpu.VMEM((devices, rows, 2 * length), jnp.bfloat16),
            pltpu.VMEM((total, period, length), jnp.float32),
            pltpu.VMEM((16, length), jnp.bfloat16),
            pltpu.VMEM((length, 2 * length), jnp.bfloat16),
            pltpu.SMEM((2 * total,), jnp.int32),
            pltpu.SMEM((total,), jnp.float32),
            pltpu.SMEM((total,), jnp.int32),
            sems(6), sems(devices), sems(5),
            sems(devices), sems(devices), sems(devices + 2), sems(devices + 2),
        ],
        compiler_params=pltpu.CompilerParams(collective_id=0, has_side_effects=True, vmem_limit_bytes=16 << 20),
        name="gather",
    )(defocus, tilts, assignment, volumes, table)


def reduce_kernel(
    side, scale, g_ref, vol_ref, sc_ref, counts_ref, new_ref, scores_ref,
    from_pair, came, going, across, down,
    pair_send, pair_recv, ring_send, ring_recv, across_send, across_recv, down_send, down_recv,
):
    devices, rows, length = g_ref.shape
    depth = devices // 2
    far = depth // 2
    me = lax.axis_index("batch")
    z, core = me // 2, me % 2
    other = 1 - core
    partner = z * 2 + other
    c = lax.axis_index("cls")
    y, x = c // side, c % side
    in_row = [y * side + (x + d) % side for d in range(1, side)]
    in_column = [((y + d) % side) * side + x for d in range(1, side)]

    def at_distance(way, d):
        return (z + d) % depth if way == 0 else (z + depth - d) % depth

    barrier = pltpu.get_barrier_semaphore()
    for way, d in ((0, 1), (1, 1), (0, 2), (1, 2)):
        peer = at_distance(way, d) * 2 + core
        pl.semaphore_signal(barrier, inc=1, device_id={"batch": peer}, device_id_type=MESH)
    pl.semaphore_signal(barrier, inc=1, device_id={"batch": partner}, device_id_type=MESH)
    for peer in in_row + in_column:
        pl.semaphore_signal(barrier, inc=1, device_id={"cls": peer}, device_id_type=MESH)
    across[0] = lax.dot_general(
        jnp.full((8, length), scale, jnp.float32), sc_ref[...], (((1,), (1,)), ((), ())),
        precision=lax.Precision.HIGHEST, preferred_element_type=jnp.float32,
    )
    pl.semaphore_wait(barrier, 5 + 2 * (side - 1))

    order = [far]
    for d in range(far - 1, 0, -1):
        order += [d, depth - d]
    order.append(0)
    pairs = {}
    for i, d in enumerate(order):
        j = (z + d) % depth
        pairs[d] = pltpu.make_async_remote_copy(
            src_ref=g_ref.at[2 * j + other], dst_ref=from_pair.at[j],
            send_sem=pair_send.at[i], recv_sem=pair_recv.at[i],
            device_id={"batch": partner}, device_id_type=MESH,
        )
        pairs[d].start()

    def spread(ref, send, recv, peers, axis):
        copies = []
        for d, peer in enumerate(peers, 1):
            copies.append(pltpu.make_async_remote_copy(
                src_ref=ref.at[0], dst_ref=ref.at[d], send_sem=send.at[d - 1], recv_sem=recv.at[d - 1],
                device_id={axis: peer}, device_id_type=MESH,
            ))
            copies[-1].start()
        return copies

    row_copies = spread(across, across_send, across_recv, in_row, "cls")

    spans = (pl.ds(0, rows // 2), pl.ds(rows // 2, rows // 2))

    def mine(j, h):
        return g_ref[2 * j + core, spans[h], :].astype(jnp.float32) + from_pair[j, spans[h], :].astype(jnp.float32)

    def ring(way, d, h):
        i = (way * far + d - 1) * 2 + h
        return pltpu.make_async_remote_copy(
            src_ref=going.at[way, d - 1, spans[h]], dst_ref=came.at[way, d - 1, spans[h]],
            send_sem=ring_send.at[i], recv_sem=ring_recv.at[i],
            device_id={"batch": at_distance(way, d if d < 3 else d - 2) * 2 + core}, device_id_type=MESH,
        )

    sent = []

    def send(way, d, h, value):
        going[way, d - 1, spans[h], :] = value.astype(jnp.bfloat16)
        sent.append(ring(way, d, h))
        sent[-1].start()

    def landed(way, d, h):
        ring(way, d, h).wait_recv()
        return came[way, d - 1, spans[h], :].astype(jnp.float32)

    pairs[far].wait_recv()
    for way in (0, 1):
        send(way, far, way, mine(at_distance(way, far), way))
    for d in (3, 1):
        if d == 1:
            for copy in row_copies:
                copy.wait_recv()
            down[0] = sum(across[d] for d in range(1, side)) + across[0]
            column_copies = spread(down, down_send, down_recv, in_column, "cls")
        for way in (0, 1):
            pairs[d if way == 0 else depth - d].wait_recv()
            for h in (0, 1):
                send(way, d, h, mine(at_distance(way, d), h))
        if d == 3:
            for way in (0, 1):
                pairs[2 if way == 0 else depth - 2].wait_recv()
    for h in (0, 1):
        for way in (0, 1):
            value = mine(at_distance(way, 2), h) + landed(way, 3, h)
            if h == way:
                value += landed(way, far, h)
            send(way, 2, h, value)

    lane = lax.broadcasted_iota(jnp.int32, (1, length), 1)
    count = jnp.sum(jnp.where(lane == me, counts_ref[0:1, :], 0.0), axis=1, keepdims=True)
    factor = STEP / (count + 1.0)
    pairs[0].wait_recv()
    for h in (0, 1):
        value = mine(z, h)
        for d in (1, 2):
            for way in (0, 1):
                value += landed(way, d, h)
        new_ref[0, spans[h], :] = vol_ref[0, spans[h], :].astype(jnp.float32) + value * factor
    for copy in column_copies:
        copy.wait_recv()
    scores_ref[...] = (sum(down[d] for d in range(1, side)) + down[0])[0:1, :]
    for copy in sent + row_copies + column_copies + list(pairs.values()):
        copy.wait_send()


def reduce_call(g, volumes, partial, counts, scale, lanes):
    devices, rows, length = g.shape
    depth = devices // 2
    far = depth // 2
    side = math.isqrt(lanes)
    inside = pl.BlockSpec(memory_space=pltpu.VMEM)
    sems = lambda n: pltpu.SemaphoreType.DMA((n,))
    peers = max(side - 1, 1)
    return pl.pallas_call(
        functools.partial(reduce_kernel, side, scale),
        out_shape=(
            jax.ShapeDtypeStruct((1, rows, length), jnp.float32),
            jax.ShapeDtypeStruct((1, partial.shape[0]), jnp.float32),
        ),
        in_specs=[inside] * 4,
        out_specs=(inside, inside),
        scratch_shapes=[
            pltpu.VMEM((depth, rows, length), jnp.bfloat16),
            pltpu.VMEM((2, far, rows, length), jnp.bfloat16),
            pltpu.VMEM((2, far, rows, length), jnp.bfloat16),
            pltpu.VMEM((side, 8, partial.shape[0]), jnp.float32),
            pltpu.VMEM((side, 8, partial.shape[0]), jnp.float32),
            sems(depth), sems(depth), sems(4 * far), sems(4 * far),
            sems(peers), sems(peers), sems(peers), sems(peers),
        ],
        compiler_params=pltpu.CompilerParams(collective_id=1, has_side_effects=True, vmem_limit_bytes=12 << 20),
        name="reduce",
    )(g, volumes, partial, counts)


def main_kernel(
    x_ref, a_ref, spec_ref, table_ref, class_in, orient_in, g_ref, sc_ref,
    v_ref, acc_ref, fwd_ref, high_ref, low_ref, cls_ref, ori_ref, sem,
):
    step = pl.program_id(0)
    block, rows, length = x_ref.shape
    classes = spec_ref.shape[0]
    period = a_ref.shape[1]
    unit = length // ORIENTS

    @pl.when(step == 0)
    def _():
        copies = [
            pltpu.make_async_copy(table_ref.at[:, pl.ds(0, 2 * length)], fwd_ref, sem.at[0]),
            pltpu.make_async_copy(table_ref.at[:, pl.ds(2 * length, length)], high_ref, sem.at[1]),
            pltpu.make_async_copy(table_ref.at[:, pl.ds(3 * length, length)], low_ref, sem.at[2]),
            pltpu.make_async_copy(class_in, cls_ref, sem.at[3]),
            pltpu.make_async_copy(orient_in, ori_ref, sem.at[4]),
        ]
        for copy in copies:
            copy.start()

        @pl.loop(0, classes)
        def _(k):
            v_ref[k] = spec_ref[k].astype(jnp.float32)
            acc_ref[k] = jnp.zeros(acc_ref.shape[1:], jnp.float32)

        for copy in copies:
            copy.wait()

    for i in range(block):
        p = step * block + i
        k = cls_ref[p]
        start = pl.multiple_of(length - unit * ori_ref[p], unit)
        y = jnp.dot(x_ref[i], fwd_ref[pl.ds(start, length), :], preferred_element_type=jnp.float32)
        totals = {}
        for r in range(0, period, 8):
            a = a_ref[i, r : r + 8, :]
            for j in range(r, rows, period):
                for c in (0, length):
                    d = y[j : j + 8, c : c + length] - a * v_ref[k, j : j + 8, c : c + length]
                    key = (j // period % 2, c)
                    totals[key] = totals[key] + d * d if key in totals else d * d
                    acc_ref[k, j : j + 8, c : c + length] += a * d
        total = sum(totals.values())
        sc_ref[i, :] = jnp.sum(total, axis=0)

    @pl.when(step == pl.num_programs(0) - 1)
    def _():
        @pl.loop(0, classes)
        def _(k):
            s = acc_ref[k]
            s_high = s.astype(jnp.bfloat16)
            s_low = (s - s_high.astype(jnp.float32)).astype(jnp.bfloat16)
            g = jnp.dot(s_high, high_ref[...], preferred_element_type=jnp.float32)
            g += jnp.dot(s_low, high_ref[...], preferred_element_type=jnp.float32)
            g += jnp.dot(s_high, low_ref[...], preferred_element_type=jnp.float32)
            g_ref[k] = g.astype(jnp.bfloat16)


def main_call(x, a, spectra, assignment, orientation, table):
    total, rows, length = x.shape
    classes = spectra.shape[0]
    period = a.shape[1]
    outside = pl.BlockSpec(memory_space=pltpu.HBM)
    return pl.pallas_call(
        main_kernel,
        out_shape=(
            jax.ShapeDtypeStruct((classes, rows, length), jnp.bfloat16),
            jax.ShapeDtypeStruct((total, length), jnp.float32),
        ),
        grid=(total // BLOCK,),
        in_specs=[
            pl.BlockSpec((BLOCK, rows, length), lambda i: (i, 0, 0)),
            pl.BlockSpec((BLOCK, period, length), lambda i: (i, 0, 0)),
            pl.BlockSpec((classes, rows, 2 * length), lambda i: (0, 0, 0)),
            outside, outside, outside,
        ],
        out_specs=[
            pl.BlockSpec((classes, rows, length), lambda i: (0, 0, 0)),
            pl.BlockSpec((BLOCK, length), lambda i: (i, 0)),
        ],
        scratch_shapes=[
            pltpu.VMEM((classes, rows, 2 * length), jnp.float32),
            pltpu.VMEM((classes, rows, 2 * length), jnp.float32),
            pltpu.VMEM((2 * length, 2 * length), jnp.bfloat16),
            pltpu.VMEM((2 * length, length), jnp.bfloat16),
            pltpu.VMEM((2 * length, length), jnp.bfloat16),
            pltpu.SMEM((total,), jnp.int32),
            pltpu.SMEM((total,), jnp.int32),
            pltpu.SemaphoreType.DMA((5,)),
        ],
        compiler_params=pltpu.CompilerParams(
            vmem_limit_bytes=44 << 20
        ),
        name="main",
    )(x, a, spectra, table, assignment, orientation)


def local(particles, volumes, assignment, defocus, tilt_limits, orientation):
    total, rows, length = particles.shape
    devices = lax.axis_size("batch")
    lanes = lax.axis_size("cls")
    assert volumes.shape[0] == 1 and rows % (length // 2) == 0
    table = tables(length)
    tilt_limits = tilt_limits.T.reshape(2 * total)
    hbm = lambda v: pltpu.with_memory_space_constraint(v, pltpu.HBM)
    volumes, assignment, defocus, tilt_limits, table, orientation, particles = map(
        hbm, (volumes, assignment, defocus, tilt_limits, table, orientation, particles)
    )
    spectra, a, tally = gather_call(volumes, assignment, defocus, tilt_limits, table, devices)
    g, partial = main_call(particles, a, spectra, assignment, orientation, table)
    scale = 1.0 / (rows * lanes * length * length)
    updated, scores = reduce_call(g, volumes, partial, tally, scale, lanes)
    return updated, scores.reshape(total)


def solution(mesh):
    in_specs = (
        P("batch", "cls", None),
        P("batch", "cls", None),
        P("batch"),
        P("batch"),
        P("batch", None),
        P("batch"),
    )
    out_specs = (P("batch", "cls", None), P("batch"))
    return jax.shard_map(local, mesh=mesh, in_specs=in_specs, out_specs=out_specs, check_vma=False)
```
